128 devices in a mesh: az: 16 (over x_lo, z, core), el: 8 (over x_hi, y).
Axes of the slice: x: 4 (x_hi: 2, x_lo: 2; x = x_hi * 2 + x_lo), y: 4, z: 4, core: 2. Of those that a mesh axis runs over, the one named last changes fastest.
Arguments:
- points: bfloat16 [16, 4096, 256], P('el', 'az'), may hold values from -6 to 6
- skip: bfloat16 [16, 4096, 256], P('el', 'az'), may hold values from -6 to 6
- tokens: bfloat16 [16, 8, 128, 256], P('az', 'el')
- send_slots: int32 [16, 8, 5, 8, 16], P('az', 'el'), may hold values from 0 to 127
- recv_idx: int32 [16, 4096, 16], P('el', 'az'), may hold values from 0 to 639, as said below
- w_query: bfloat16 [256, 256], replicated, may hold values from -0.375 to 0.375
- w_key: bfloat16 [256, 256], replicated, may hold values from -0.375 to 0.375
- w_value: bfloat16 [256, 256], replicated, may hold values from -0.375 to 0.375
- w_out: bfloat16 [256, 256], replicated, may hold values from -0.375 to 0.375
- w_hid: bfloat16 [256, 1024], replicated, may hold values from -0.375 to 0.375
- w_skip: bfloat16 [256, 1024], replicated, may hold values from -0.375 to 0.375
- w_down: bfloat16 [1024, 256], replicated, may hold values from -0.1875 to 0.1875
- w_conv: bfloat16 [9, 256, 256], replicated, may hold values from -0.125 to 0.125
Outputs:
- refined: bfloat16 [16, 4096, 256], P('el', 'az')
The draws below stay inside these ranges and needn't reach their ends.
Inputs may be any that keep to these rules, and one draw needn't show every extreme that they name: send_slots[o, e, j, f, k] is the row of owner device (o, e)'s tokens sent as slot k to the device of azimuth block (o + j - 2) mod 16 and elevation block f. `recv_idx`: an entry (j * 8 + e) * 16 + k names slot k of what the device of elevation block e, 2 - j azimuth blocks away, sends to the point's device. For each requesting device and each such owner only the slots below a live count of 1 to 16 are named; each requesting device has its own block's slots from itself all live.
All inputs are finite; a program needn't handle non-finite values.
Results may differ from the reference program's by a relative error of at most 0.01.
Values may be sent and summed in bfloat16 or wider, within the bound.
A program may use at most 64 MiB of HBM per device.

```python
import math
import jax
import jax.numpy as jnp
from jax import lax

D = 256
HEADS = 8
FF = 1024
NEAR = 16
REACH = 2
R_DEV = 2
C_DEV = 256
TOK_DEV = 128
CAP = 16
OFFSETS = 5
AZ_BLOCKS = 16
EL_BLOCKS = 8
ROWS = 16
COLS = 4096


def draw_tokens(key, part):
    shape = (AZ_BLOCKS, EL_BLOCKS, TOK_DEV, D)
    first = jax.random.fold_in(key, 0)
    return jax.random.normal(first, shape, jnp.float32).astype(jnp.bfloat16)


def draw_recv_idx(key, part):
    keys = jax.random.split(key, 4)
    live_counts = jax.random.randint(keys[0], (EL_BLOCKS, AZ_BLOCKS, OFFSETS, EL_BLOCKS), 1, CAP + 1)
    own_group = (jnp.arange(OFFSETS)[None, None, :, None] == REACH) & (jnp.arange(EL_BLOCKS)[:, None, None, None] == jnp.arange(EL_BLOCKS)[None, None, None, :])
    live_counts = jnp.where(own_group, CAP, live_counts)
    shape = (ROWS, COLS, NEAR)
    group = jax.random.randint(keys[1], shape, 0, OFFSETS)
    source_el = jax.random.randint(keys[2], shape, 0, EL_BLOCKS)
    raw_slot = jax.random.randint(keys[3], shape, 0, 1 << 20)
    target_el = (jnp.arange(ROWS) // R_DEV)[:, None, None]
    column_block = (jnp.arange(COLS) // C_DEV)[None, :, None]
    limit = live_counts[target_el, column_block, group, source_el]
    slot_number = raw_slot % limit
    return ((group * EL_BLOCKS + source_el) * CAP + slot_number).astype(jnp.int32)


def with_ends(array, own_key, least, top_value):
    place = [jax.random.randint(jax.random.fold_in(own_key, axis), (), 0, length) for axis, length in enumerate(array.shape)]
    main_axis = array.shape.index(max(array.shape))
    beside = place[:main_axis] + [(place[main_axis] + 1) % array.shape[main_axis]] + place[main_axis + 1:]
    return array.at[tuple(place)].set(least).at[tuple(beside)].set(top_value)


def steps_of(key, shape, cuts, smallest, top_value):
    level = 1.0
    for dim, parts in cuts:
        draws = jax.random.uniform(jax.random.fold_in(jax.random.fold_in(key, 6), dim), (parts,), jnp.float32, smallest / len(cuts), top_value / len(cuts))
        level = level * jnp.repeat(jnp.exp(draws), shape[dim] // parts).reshape((-1,) + (1,) * (len(shape) - 1 - dim))
    return level


def normal_values(key, extent, width, most, cuts=(), kind=jnp.bfloat16):
    entries = jax.random.normal(key, extent, jnp.float32) * width
    if len(cuts) > 0:
        entries = steps_of(key, extent, cuts, -0.22, 0.18) * entries
    return jnp.clip(entries, min=-most, max=most).astype(kind)


def setup_inputs(seed: int = 0) -> dict:
    seeds = jax.random.split(jax.random.key(seed), 14)
    points = normal_values(seeds[0], (ROWS, COLS, D), 1.0, 6.0, ((0, 8), (1, 16)))
    skip = normal_values(seeds[1], (ROWS, COLS, D), 1.0, 6.0, ((0, 8), (1, 16)))
    tokens = draw_tokens(jax.random.fold_in(seeds[13], 71), 0)
    send_slots = with_ends(jax.random.randint(seeds[3], (AZ_BLOCKS, EL_BLOCKS, OFFSETS, EL_BLOCKS, CAP), 0, TOK_DEV), jax.random.fold_in(seeds[3], 1), 0, TOK_DEV - 1).astype(jnp.int32)
    recv_idx = draw_recv_idx(jax.random.fold_in(seeds[13], 71), 0)
    w_query = normal_values(seeds[5], (D, D), D ** -0.5, 0.375)
    w_key = normal_values(seeds[6], (D, D), D ** -0.5, 0.375)
    w_value = normal_values(seeds[7], (D, D), D ** -0.5, 0.375)
    w_out = normal_values(seeds[8], (D, D), D ** -0.5, 0.375)
    w_hid = normal_values(seeds[9], (D, FF), D ** -0.5, 0.375)
    w_skip = normal_values(seeds[10], (D, FF), D ** -0.5, 0.375)
    w_down = normal_values(seeds[11], (FF, D), FF ** -0.5, 0.1875)
    w_conv = normal_values(seeds[12], (9, D, D), (9 * D) ** -0.5, 0.125)
    return dict(points=points, skip=skip, tokens=tokens, send_slots=send_slots, recv_idx=recv_idx, w_query=w_query, w_key=w_key, w_value=w_value, w_out=w_out, w_hid=w_hid, w_skip=w_skip, w_down=w_down, w_conv=w_conv)


def normalize(features):
    widened = features.astype(jnp.float32)
    return widened * lax.rsqrt(lax.optimization_barrier(jnp.mean(widened * widened, axis=-1, keepdims=True)) + 1e-06)

def reference(points, skip, tokens, send_slots, recv_idx, w_query, w_key, w_value, w_out, w_hid, w_skip, w_down, w_conv):
    flat_tokens = tokens.reshape(AZ_BLOCKS * EL_BLOCKS * TOK_DEV, D)
    key_rows = jnp.dot(flat_tokens, w_key, preferred_element_type=jnp.float32).astype(jnp.bfloat16)
    normed_tokens = normalize(flat_tokens).astype(jnp.bfloat16)
    value_rows = jnp.dot(normed_tokens, w_value, preferred_element_type=jnp.float32).astype(jnp.bfloat16)
    head_width = D // HEADS
    scale_factor = 1.0 / math.sqrt(head_width)
    column_block = jnp.arange(COLS, dtype=jnp.int32) // C_DEV

    def one_row(inputs):
        point_row, skip_row, index_row, row_number = inputs
        group = index_row // (EL_BLOCKS * CAP)
        source_el = index_row // CAP % EL_BLOCKS
        slot_number = index_row % CAP
        owner = (column_block[:, None] - group + REACH) % AZ_BLOCKS
        target_el = row_number // R_DEV
        local_row = send_slots[owner, source_el, group, target_el, slot_number]
        token_id = ((owner * EL_BLOCKS + source_el) * TOK_DEV + local_row).astype(jnp.int32)
        picked_keys = jnp.take(key_rows, token_id, axis=0).reshape(COLS, NEAR, HEADS, head_width)
        picked_values = jnp.take(value_rows, token_id, axis=0).reshape(COLS, NEAR, HEADS, head_width)
        query = jnp.dot(point_row, w_query, preferred_element_type=jnp.float32).astype(jnp.bfloat16)
        query = query.reshape(COLS, HEADS, head_width)
        scores = jnp.einsum('bhd,bkhd->bhk', query.astype(jnp.float32), picked_keys.astype(jnp.float32)) * scale_factor
        shifted = jnp.exp(scores - lax.optimization_barrier(jnp.max(scores, axis=-1, keepdims=True)))
        weights = (shifted / lax.optimization_barrier(jnp.sum(shifted, axis=-1, keepdims=True))).astype(jnp.bfloat16)
        combined = jnp.einsum('bhk,bkhd->bhd', weights.astype(jnp.float32), picked_values.astype(jnp.float32))
        attended = combined.reshape(COLS, D).astype(jnp.bfloat16)
        residual_sum = point_row.astype(jnp.float32) + jnp.dot(attended, w_out, preferred_element_type=jnp.float32)
        normed = normalize(residual_sum).astype(jnp.bfloat16)
        hidden_pre = jnp.dot(normed, w_hid, preferred_element_type=jnp.float32) + jnp.dot(skip_row, w_skip, preferred_element_type=jnp.float32)
        inner = jax.nn.gelu(hidden_pre, approximate=True).astype(jnp.bfloat16)
        return residual_sum + jnp.dot(inner, w_down, preferred_element_type=jnp.float32)
    joined = lax.map(one_row, (points, skip, recv_idx, jnp.arange(ROWS, dtype=jnp.int32)))
    conv_input = normalize(joined).astype(jnp.bfloat16)
    widened = jnp.concatenate([conv_input[:, -1:], conv_input, conv_input[:, :1]], axis=1)
    padded = jnp.pad(widened, ((1, 1), (0, 0), (0, 0)))
    refined = joined
    for tap_index in range(9):
        row_step = tap_index // 3
        col_step = tap_index % 3
        window = padded[row_step:row_step + ROWS, col_step:col_step + COLS].reshape(ROWS * COLS, D)
        refined = refined + jnp.dot(window, w_conv[tap_index], preferred_element_type=jnp.float32).reshape(ROWS, COLS, D)
    return refined.astype(jnp.bfloat16)
```

```python
import math

import jax
import jax.numpy as jnp
from jax import lax
from jax.experimental import pallas as pl
from jax.experimental.pallas import tpu as pltpu
from jax.sharding import PartitionSpec as P

D = 256
HEADS = 8
HEAD = D // HEADS
FF = 1024
NEAR = 16
REACH = 2
OFFSETS = 5
CAP = 16
TOK = 128
COLS = 256
EL = 8
AZ = 16
SLOTS = OFFSETS * EL
TABLE = SLOTS * CAP
POINTS = 512
HALF = 256
PAD = 16
FAR = -1e30
MESH = pl.DeviceIdType.MESH
BF16 = jnp.bfloat16
F32 = jnp.float32

SEGMENTS = (
    (0, 0, 0, 64, 0),
    (0, 0, 192, 64, 64),
    (0, 1, 0, 64, 128),
    (0, 1, 192, 64, 192),
    (1, 0, 64, 128, 0),
    (1, 1, 64, 128, 128),
)


def nt(a, b):
    return lax.dot_general(a, b, (((1,), (1,)), ((), ())), preferred_element_type=F32)


def nn(a, b):
    return lax.dot_general(a, b, (((1,), (0,)), ((), ())), preferred_element_type=F32)


def inv_rms(x):
    return lax.rsqrt(jnp.mean(x * x, axis=-1, keepdims=True) + 1e-06)


def gelu(u):
    inner = math.sqrt(2.0 / math.pi) * (u + 0.044715 * (u * u * u))
    return 0.5 * u * (1.0 + jnp.tanh(inner))


def kernel(
    points_hbm,
    skip_hbm,
    tokens_hbm,
    slots_hbm,
    index_hbm,
    wq_hbm,
    wk_hbm,
    wv_hbm,
    wo_hbm,
    wh_hbm,
    ws_hbm,
    wd_hbm,
    wc_hbm,
    out_ref,
    pts,
    skp,
    tok,
    slt,
    idx,
    wq,
    wk,
    wv,
    wo,
    wh,
    ws,
    wd,
    wc,
    payload,
    recv,
    qmt,
    hs,
    bias,
    kbuf,
    vt,
    att,
    joined,
    cin,
    wvt,
    in_sem,
    send_sem,
    recv_sem,
    halo_send,
    halo_recv,
):
    az = lax.axis_index("az")
    el = lax.axis_index("el")

    def az_at(step):
        return lax.rem(az + step + AZ, AZ)

    def el_at(step):
        return lax.rem(el + step, EL)

    def load(number, src, dst):
        copy = pltpu.make_async_copy(src, dst, in_sem.at[number])
        copy.start()
        return copy

    tok_in = load(0, tokens_hbm.at[0, 0], tok)
    slt_in = load(1, slots_hbm.at[0, 0], slt)
    wq_in = load(2, wq_hbm, wq)
    pts_in = []
    idx_in = []
    skp_in = []
    for number, (chunk, row, col, width, place) in enumerate(SEGMENTS):
        here = pl.ds(chunk * HALF + place, width)
        pts_in.append(load(3 + number, points_hbm.at[row, pl.ds(col, width)], pts.at[here]))
        idx_in.append(load(9 + number, index_hbm.at[row, pl.ds(col, width)], idx.at[here]))
    for number, (chunk, row, col, width, place) in enumerate(SEGMENTS):
        here = pl.ds(chunk * HALF + place, width)
        skp_in.append(load(15 + number, skip_hbm.at[row, pl.ds(col, width)], skp.at[here]))
    ws_in = load(21, ws_hbm, ws)
    wk_in = load(22, wk_hbm, wk)
    wv_in = load(23, wv_hbm, wv)
    wo_in = load(24, wo_hbm, wo)
    wh_in = load(25, wh_hbm, wh)
    wd_in = load(26, wd_hbm, wd)
    wc_in = load(27, wc_hbm, wc)

    barrier = pltpu.get_barrier_semaphore()

    def greet(number, carry):
        j = lax.div(number, EL)
        r = lax.rem(number, EL)

        @pl.when(number != REACH * EL)
        def _():
            pl.semaphore_signal(
                barrier,
                inc=1,
                device_id={"az": az_at(j - REACH), "el": el_at(r)},
                device_id_type=MESH,
            )

        return carry

    lax.fori_loop(0, SLOTS, greet, 0)

    slt_in.wait()
    tok_in.wait()
    eye = (
        lax.broadcasted_iota(jnp.int32, (NEAR, NEAR), 0)
        == lax.broadcasted_iota(jnp.int32, (NEAR, NEAR), 1)
    ).astype(F32).astype(BF16)
    slot_cols = nt(eye, slt[...].reshape(SLOTS, CAP).astype(F32).astype(BF16))
    lane_id = lax.broadcasted_iota(jnp.int32, (CAP, TOK), 1).astype(F32)
    picks = jnp.concatenate(
        [
            (jnp.broadcast_to(slot_cols[:, s : s + 1], (CAP, TOK)) == lane_id)
            .astype(F32)
            .astype(BF16)
            for s in range(SLOTS)
        ],
        axis=0,
    )
    payload[...] = nn(picks, tok[...]).astype(BF16).reshape(SLOTS, CAP, D)

    wq_in.wait()
    for copy in pts_in:
        copy.wait()
    query_t = (nt(wq[...].T, pts[...]) * (1.0 / math.sqrt(HEAD) / math.log(2.0))).astype(BF16)
    zero_rows = jnp.zeros((HEAD, POINTS), BF16)
    for h in range(HEADS):
        for part in range(4):
            rows = pl.ds(part * HEAD, HEAD)
            if part == h % 4:
                qmt[h, rows, :] = query_t[h * HEAD : (h + 1) * HEAD, :]
            else:
                qmt[h, rows, :] = zero_rows

    pl.semaphore_wait(barrier, SLOTS - 1)

    def token_copy(j, r):
        f = el_at(r)
        return pltpu.make_async_remote_copy(
            src_ref=payload.at[j * EL + f],
            dst_ref=recv.at[j * EL + el],
            send_sem=send_sem.at[j * EL + f],
            recv_sem=recv_sem.at[j * EL + el],
            device_id={"az": az_at(j - REACH), "el": f},
            device_id_type=MESH,
        )

    for r in (4, 6, 2, 5, 7, 3, 1, 0):
        for j in range(OFFSETS):
            if (j, r) != (REACH, 0):
                token_copy(j, r).start()
    recv[REACH * EL + el] = payload[REACH * EL + el]

    for copy in idx_in:
        copy.wait()
    entries = idx[...]
    low = nt(eye, (entries & (TOK - 1)).astype(F32).astype(BF16)).astype(jnp.int32)
    high = nt(eye, lax.shift_right_logical(entries, 7).astype(F32).astype(BF16)).astype(jnp.int32)
    unit = lax.shift_left(jnp.ones_like(high), high * 5)

    down = lax.broadcasted_iota(jnp.int32, (8, POINTS), 0)
    for block in range(TOK // 8):
        total = jnp.zeros((8, POINTS), jnp.int32)
        for n in range(NEAR):
            hit = jnp.broadcast_to(low[n : n + 1, :] - block * 8, (8, POINTS)) == down
            total = total + jnp.where(hit, jnp.broadcast_to(unit[n : n + 1, :], (8, POINTS)), 0)
        for group in range(OFFSETS):
            count = lax.shift_right_logical(total, 5 * group) & 31
            logs = jnp.log(count.astype(F32)) * (1.0 / math.log(2.0))
            bias[pl.ds(group * TOK + block * 8, 8), :] = jnp.where(count > 0, logs, FAR)

    for copy in skp_in:
        copy.wait()
    ws_in.wait()
    for block in range(FF // D):
        cols = pl.ds(block * D, D)
        hs[:, cols] = nn(skp[...], ws[:, cols])

    wv_in.wait()
    wvt[...] = wv[...].T
    vt[:, pl.ds(HEAD, 16), :] = jnp.ones((HEADS, 16, TABLE), BF16)

    @pl.when(el == 0)
    def _():
        cin[0, :, :] = jnp.zeros((COLS + 2 * PAD, D), BF16)

    @pl.when(el == EL - 1)
    def _():
        cin[3, :, :] = jnp.zeros((COLS + 2 * PAD, D), BF16)

    wk_in.wait()
    for j in range(OFFSETS):
        for r in range(EL):
            if (j, r) != (REACH, 0):
                e = el_at(r)
                pltpu.make_async_remote_copy(
                    src_ref=payload.at[j * EL + e],
                    dst_ref=recv.at[j * EL + e],
                    send_sem=send_sem.at[j * EL + e],
                    recv_sem=recv_sem.at[j * EL + e],
                    device_id={"az": az_at(REACH - j), "el": e},
                    device_id_type=MESH,
                ).wait_recv()
    rows = recv[...].reshape(TABLE, D)
    kbuf[...] = nn(rows, wk[...]).astype(BF16)
    wide = rows.astype(F32)
    normed_tokens = (wide * inv_rms(wide)).astype(BF16)
    value_t = nt(wvt[...], normed_tokens).astype(BF16)
    for h in range(HEADS):
        vt[h, pl.ds(0, HEAD), :] = value_t[h * HEAD : (h + 1) * HEAD, :]

    wo_in.wait()
    wh_in.wait()
    wd_in.wait()

    def halo(number, src, dst, device):
        return pltpu.make_async_remote_copy(
            src_ref=src,
            dst_ref=dst,
            send_sem=halo_send.at[number],
            recv_sem=halo_recv.at[number],
            device_id=device,
            device_id_type=MESH,
        )

    here = {"az": az, "el": el}
    west, east = az_at(-1), az_at(1)
    above = jnp.maximum(el - 1, 0)
    below = jnp.minimum(el + 1, EL - 1)
    first, last = pl.ds(PAD, PAD), pl.ds(COLS, PAD)
    left_pad, right_pad = pl.ds(0, PAD), pl.ds(PAD + COLS, PAD)

    def up_copies(chunk):
        if chunk == 1:
            mid = pl.ds(PAD + 64, 128)
            return [halo(0, cin.at[1, mid], cin.at[3, mid], {"az": az, "el": above})]
        one, two = pl.ds(PAD, 64), pl.ds(PAD + 192, 64)
        return [
            halo(1, cin.at[1, one], cin.at[3, one], {"az": az, "el": above}),
            halo(2, cin.at[1, two], cin.at[3, two], {"az": az, "el": above}),
            halo(3, cin.at[1, first], cin.at[3, right_pad], {"az": west, "el": above}),
            halo(4, cin.at[1, last], cin.at[3, left_pad], {"az": east, "el": above}),
        ]

    def down_copies(chunk):
        if chunk == 1:
            mid = pl.ds(PAD + 64, 128)
            return [halo(5, cin.at[2, mid], cin.at[0, mid], {"az": az, "el": below})]
        one, two = pl.ds(PAD, 64), pl.ds(PAD + 192, 64)
        return [
            halo(6, cin.at[2, one], cin.at[0, one], {"az": az, "el": below}),
            halo(7, cin.at[2, two], cin.at[0, two], {"az": az, "el": below}),
            halo(8, cin.at[2, first], cin.at[0, right_pad], {"az": west, "el": below}),
            halo(9, cin.at[2, last], cin.at[0, left_pad], {"az": east, "el": below}),
        ]

    def side_copies():
        return [
            halo(10, cin.at[1, first], cin.at[1, right_pad], {"az": west, "el": el}),
            halo(11, cin.at[2, first], cin.at[2, right_pad], {"az": west, "el": el}),
            halo(12, cin.at[1, last], cin.at[1, left_pad], {"az": east, "el": el}),
            halo(13, cin.at[2, last], cin.at[2, left_pad], {"az": east, "el": el}),
        ]

    for chunk in range(2):
        span = pl.ds(chunk * HALF, HALF)
        for h in range(HEADS):
            lanes = pl.ds((h // 4) * 128, 128)
            scores = nn(kbuf[:, lanes], qmt[h, :, span]) + bias[:, span]
            top = jnp.max(scores, axis=0, keepdims=True)
            weights = jnp.exp2((scores - top).astype(BF16))
            summed = nn(vt[h], weights)
            share = summed[:HEAD, :] * (1.0 / summed[HEAD : HEAD + 1, :])
            att[pl.ds(h * HEAD, HEAD), :] = share
        attended = att[...].T.astype(BF16)
        residual = pts[span, :].astype(F32) + nn(attended, wo[...])
        normed = (residual * inv_rms(residual)).astype(BF16)
        total = residual
        for block in range(FF // D):
            cols = pl.ds(block * D, D)
            hidden = gelu(nn(normed, wh[:, cols]) + hs[span, cols]).astype(BF16)
            total = total + nn(hidden, wd[cols, :])
        conv_in = (total * inv_rms(total)).astype(BF16)
        for c, row, col, width, place in SEGMENTS:
            if c == chunk:
                joined[row, pl.ds(col, width), :] = total[place : place + width, :]
                cin[1 + row, pl.ds(PAD + col, width), :] = conv_in[place : place + width, :]

        @pl.when(el > 0)
        def _():
            for copy in up_copies(chunk):
                copy.start()

        @pl.when(el < EL - 1)
        def _():
            for copy in down_copies(chunk):
                copy.start()

        if chunk == 0:
            for copy in side_copies():
                copy.start()

    for copy in side_copies():
        copy.wait_recv()
    wc_in.wait()

    def taps(row):
        return [cin[row, pl.ds(PAD + step, COLS), :] for step in (-1, 0, 1)]

    own = jnp.concatenate(taps(1) + taps(2), axis=1)
    upper = joined[0] + nn(own, wc[pl.ds(3, 6)].reshape(6 * D, D))
    lower = joined[1] + nn(own, wc[pl.ds(0, 6)].reshape(6 * D, D))

    @pl.when(el > 0)
    def _():
        for chunk in range(2):
            for copy in down_copies(chunk):
                copy.wait_recv()

    @pl.when(el < EL - 1)
    def _():
        for chunk in range(2):
            for copy in up_copies(chunk):
                copy.wait_recv()

    upper = upper + nn(jnp.concatenate(taps(0), axis=1), wc[pl.ds(0, 3)].reshape(3 * D, D))
    lower = lower + nn(jnp.concatenate(taps(3), axis=1), wc[pl.ds(6, 3)].reshape(3 * D, D))
    out_ref[0] = upper.astype(BF16)
    out_ref[1] = lower.astype(BF16)

    for j in range(OFFSETS):
        for r in range(EL):
            if (j, r) != (REACH, 0):
                token_copy(j, r).wait_send()
    for copy in side_copies():
        copy.wait_send()

    @pl.when(el > 0)
    def _():
        for chunk in range(2):
            for copy in up_copies(chunk):
                copy.wait_send()

    @pl.when(el < EL - 1)
    def _():
        for chunk in range(2):
            for copy in down_copies(chunk):
                copy.wait_send()


def per_device(*args):
    any_spec = pl.BlockSpec(memory_space=pl.ANY)
    return pl.pallas_call(
        kernel,
        out_shape=jax.ShapeDtypeStruct((2, COLS, D), BF16),
        in_specs=[any_spec] * len(args),
        out_specs=pl.BlockSpec(memory_space=pltpu.VMEM),
        scratch_shapes=[
            pltpu.VMEM((POINTS, D), BF16),
            pltpu.VMEM((POINTS, D), BF16),
            pltpu.VMEM((TOK, D), BF16),
            pltpu.VMEM((OFFSETS, EL, CAP), jnp.int32),
            pltpu.VMEM((POINTS, NEAR), jnp.int32),
            pltpu.VMEM((D, D), BF16),
            pltpu.VMEM((D, D), BF16),
            pltpu.VMEM((D, D), BF16),
            pltpu.VMEM((D, D), BF16),
            pltpu.VMEM((D, FF), BF16),
            pltpu.VMEM((D, FF), BF16),
            pltpu.VMEM((FF, D), BF16),
            pltpu.VMEM((9, D, D), BF16),
            pltpu.VMEM((SLOTS, CAP, D), BF16),
            pltpu.VMEM((SLOTS, CAP, D), BF16),
            pltpu.VMEM((HEADS, D // 2, POINTS), BF16),
            pltpu.VMEM((POINTS, FF), F32),
            pltpu.VMEM((TABLE, POINTS), F32),
            pltpu.VMEM((TABLE, D), BF16),
            pltpu.VMEM((HEADS, HEAD + 16, TABLE), BF16),
            pltpu.VMEM((D, HALF), F32),
            pltpu.VMEM((2, COLS, D), F32),
            pltpu.VMEM((4, COLS + 2 * PAD, D), BF16),
            pltpu.VMEM((D, D), BF16),
            pltpu.SemaphoreType.DMA((28,)),
            pltpu.SemaphoreType.DMA((SLOTS,)),
            pltpu.SemaphoreType.DMA((SLOTS,)),
            pltpu.SemaphoreType.DMA((14,)),
            pltpu.SemaphoreType.DMA((14,)),
        ],
        compiler_params=pltpu.CompilerParams(
            collective_id=0, has_side_effects=True, vmem_limit_bytes=56 * 1024 * 1024
        ),
        name="decoder",
    )(*args)


def solution(mesh):
    return jax.shard_map(
        per_device,
        mesh=mesh,
        in_specs=(
            P("el", "az", None),
            P("el", "az", None),
            P("az", "el", None, None),
            P("az", "el", None, None, None),
            P("el", "az", None),
            P(),
            P(),
            P(),
            P(),
            P(),
            P(),
            P(),
            P(),
        ),
        out_specs=P("el", "az", None),
        check_vma=False,
    )
```

```python
import math

import jax
import jax.numpy as jnp
from jax import lax
from jax.experimental import pallas as pl
from jax.experimental.pallas import tpu as pltpu
from jax.sharding import PartitionSpec as P

D = 256
HEADS = 8
HEAD = D // HEADS
FF = 1024
NEAR = 16
REACH = 2
OFFSETS = 5
CAP = 16
TOK = 128
COLS = 256
EL = 8
AZ = 16
SLOTS = OFFSETS * EL
TABLE = SLOTS * CAP
POINTS = 512
HALF = 256
PAD = 16
FAR = -1e30
MESH = pl.DeviceIdType.MESH
BF16 = jnp.bfloat16
F32 = jnp.float32

SEGMENTS = (
    (0, 0, 0, 64, 0),
    (0, 0, 192, 64, 64),
    (0, 1, 0, 64, 128),
    (0, 1, 192, 64, 192),
    (1, 0, 64, 128, 0),
    (1, 1, 64, 128, 128),
)


def nt(a, b):
    return lax.dot_general(a, b, (((1,), (1,)), ((), ())), preferred_element_type=F32)


def nn(a, b):
    return lax.dot_general(a, b, (((1,), (0,)), ((), ())), preferred_element_type=F32)


def inv_rms(x):
    return lax.rsqrt(jnp.mean(x * x, axis=-1, keepdims=True) + 1e-06)


def gelu(u):
    inner = math.sqrt(2.0 / math.pi) * (u + 0.044715 * (u * u * u))
    return 0.5 * u * (1.0 + jnp.tanh(inner))


def kernel(
    points_hbm,
    skip_hbm,
    tokens_hbm,
    slots_hbm,
    index_hbm,
    wq_hbm,
    wk_hbm,
    wv_hbm,
    wo_hbm,
    wh_hbm,
    ws_hbm,
    wd_hbm,
    wc_hbm,
    out_ref,
    pts,
    skp,
    tok,
    slt,
    idx,
    wq,
    wk,
    wv,
    wo,
    wh,
    ws,
    wd,
    wc,
    payload,
    recv,
    qmt,
    hs,
    bias,
    kbuf,
    vt,
    att,
    joined,
    cin,
    wvt,
    in_sem,
    send_sem,
    recv_sem,
    halo_send,
    halo_recv,
):
    az = lax.axis_index("az")
    el = lax.axis_index("el")

    def az_at(step):
        return lax.rem(az + step + AZ, AZ)

    def el_at(step):
        return lax.rem(el + step, EL)

    def load(number, src, dst):
        copy = pltpu.make_async_copy(src, dst, in_sem.at[number])
        copy.start()
        return copy

    tok_in = load(0, tokens_hbm.at[0, 0], tok)
    slt_in = load(1, slots_hbm.at[0, 0], slt)
    wq_in = load(2, wq_hbm, wq)
    pts_in = []
    skp_in = []
    for number, (chunk, row, col, width, place) in enumerate(SEGMENTS):
        here = pl.ds(chunk * HALF + place, width)
        pts_in.append(load(3 + number, points_hbm.at[row, pl.ds(col, width)], pts.at[here]))
    for number, (chunk, row, col, width, place) in enumerate(SEGMENTS):
        here = pl.ds(chunk * HALF + place, width)
        skp_in.append(load(15 + number, skip_hbm.at[row, pl.ds(col, width)], skp.at[here]))
    idx_in = load(9, index_hbm, idx)
    ws_in = load(21, ws_hbm, ws)
    wk_in = load(22, wk_hbm, wk)
    wv_in = load(23, wv_hbm, wv)
    wo_in = load(24, wo_hbm, wo)
    wh_in = load(25, wh_hbm, wh)
    wd_in = load(26, wd_hbm, wd)
    wc_in = load(27, wc_hbm, wc)

    barrier = pltpu.get_barrier_semaphore()

    def greet(number, carry):
        j = lax.div(number, EL)
        r = lax.rem(number, EL)

        @pl.when(number != REACH * EL)
        def _():
            pl.semaphore_signal(
                barrier,
                inc=1,
                device_id={"az": az_at(j - REACH), "el": el_at(r)},
                device_id_type=MESH,
            )

        return carry

    lax.fori_loop(0, SLOTS, greet, 0)

    slt_in.wait()
    tok_in.wait()
    eye = (
        lax.broadcasted_iota(jnp.int32, (NEAR, NEAR), 0)
        == lax.broadcasted_iota(jnp.int32, (NEAR, NEAR), 1)
    ).astype(F32).astype(BF16)
    slot_cols = nt(eye, slt[...].reshape(SLOTS, CAP).astype(F32).astype(BF16))
    lane_id = lax.broadcasted_iota(jnp.int32, (CAP, TOK), 1).astype(F32)
    picks = jnp.concatenate(
        [
            (jnp.broadcast_to(slot_cols[:, s : s + 1], (CAP, TOK)) == lane_id)
            .astype(F32)
            .astype(BF16)
            for s in range(SLOTS)
        ],
        axis=0,
    )
    payload[...] = nn(picks, tok[...]).astype(BF16).reshape(SLOTS, CAP, D)

    wq_in.wait()
    for copy in pts_in:
        copy.wait()
    query_t = (nt(wq[...].T, pts[...]) * (1.0 / math.sqrt(HEAD) / math.log(2.0))).astype(BF16)
    zero_rows = jnp.zeros((HEAD, POINTS), BF16)
    for h in range(HEADS):
        for part in range(4):
            rows = pl.ds(part * HEAD, HEAD)
            if part == h % 4:
                qmt[h, rows, :] = query_t[h * HEAD : (h + 1) * HEAD, :]
            else:
                qmt[h, rows, :] = zero_rows

    pl.semaphore_wait(barrier, SLOTS - 1)

    def token_copy(j, r):
        f = el_at(r)
        return pltpu.make_async_remote_copy(
            src_ref=payload.at[j * EL + f],
            dst_ref=recv.at[j * EL + el],
            send_sem=send_sem.at[j * EL + f],
            recv_sem=recv_sem.at[j * EL + el],
            device_id={"az": az_at(j - REACH), "el": f},
            device_id_type=MESH,
        )

    for r in (4, 6, 2, 5, 7, 3, 1, 0):
        for j in range(OFFSETS):
            if (j, r) != (REACH, 0):
                token_copy(j, r).start()
    recv[REACH * EL + el] = payload[REACH * EL + el]

    idx_in.wait()
    entries = jnp.concatenate(
        [idx[row, :, col : col + width] for _, row, col, width, _ in SEGMENTS], axis=1
    )
    low = entries & (TOK - 1)
    high = lax.shift_right_logical(entries, 7)
    unit = lax.shift_left(jnp.ones_like(high), high * 5)

    down = lax.broadcasted_iota(jnp.int32, (8, POINTS), 0)
    for block in range(TOK // 8):
        total = jnp.zeros((8, POINTS), jnp.int32)
        for n in range(NEAR):
            hit = jnp.broadcast_to(low[n : n + 1, :] - block * 8, (8, POINTS)) == down
            total = total + jnp.where(hit, jnp.broadcast_to(unit[n : n + 1, :], (8, POINTS)), 0)
        for group in range(OFFSETS):
            count = lax.shift_right_logical(total, 5 * group) & 31
            logs = jnp.log(count.astype(F32)) * (1.0 / math.log(2.0))
            bias[pl.ds(group * TOK + block * 8, 8), :] = jnp.where(count > 0, logs, FAR)

    for copy in skp_in:
        copy.wait()
    ws_in.wait()
    for block in range(FF // D):
        cols = pl.ds(block * D, D)
        hs[:, cols] = nn(skp[...], ws[:, cols])

    wv_in.wait()
    wvt[...] = wv[...].T
    vt[:, pl.ds(HEAD, 16), :] = jnp.ones((HEADS, 16, TABLE), BF16)

    @pl.when(el == 0)
    def _():
        cin[0, :, :] = jnp.zeros((COLS + 2 * PAD, D), BF16)

    @pl.when(el == EL - 1)
    def _():
        cin[3, :, :] = jnp.zeros((COLS + 2 * PAD, D), BF16)

    wk_in.wait()
    for j in range(OFFSETS):
        for r in range(EL):
            if (j, r) != (REACH, 0):
                e = el_at(r)
                pltpu.make_async_remote_copy(
                    src_ref=payload.at[j * EL + e],
                    dst_ref=recv.at[j * EL + e],
                    send_sem=send_sem.at[j * EL + e],
                    recv_sem=recv_sem.at[j * EL + e],
                    device_id={"az": az_at(REACH - j), "el": e},
                    device_id_type=MESH,
                ).wait_recv()
    rows = recv[...].reshape(TABLE, D)
    kbuf[...] = nn(rows, wk[...]).astype(BF16)
    wide = rows.astype(F32)
    normed_tokens = (wide * inv_rms(wide)).astype(BF16)
    value_t = nt(wvt[...], normed_tokens).astype(BF16)
    for h in range(HEADS):
        vt[h, pl.ds(0, HEAD), :] = value_t[h * HEAD : (h + 1) * HEAD, :]

    wo_in.wait()
    wh_in.wait()
    wd_in.wait()

    def halo(number, src, dst, device):
        return pltpu.make_async_remote_copy(
            src_ref=src,
            dst_ref=dst,
            send_sem=halo_send.at[number],
            recv_sem=halo_recv.at[number],
            device_id=device,
            device_id_type=MESH,
        )

    here = {"az": az, "el": el}
    west, east = az_at(-1), az_at(1)
    above = jnp.maximum(el - 1, 0)
    below = jnp.minimum(el + 1, EL - 1)
    first, last = pl.ds(PAD, PAD), pl.ds(COLS, PAD)
    left_pad, right_pad = pl.ds(0, PAD), pl.ds(PAD + COLS, PAD)

    def up_copies(chunk):
        if chunk == 1:
            mid = pl.ds(PAD + 64, 128)
            return [halo(0, cin.at[1, mid], cin.at[3, mid], {"az": az, "el": above})]
        one, two = pl.ds(PAD, 64), pl.ds(PAD + 192, 64)
        return [
            halo(1, cin.at[1, one], cin.at[3, one], {"az": az, "el": above}),
            halo(2, cin.at[1, two], cin.at[3, two], {"az": az, "el": above}),
            halo(3, cin.at[1, first], cin.at[3, right_pad], {"az": west, "el": above}),
            halo(4, cin.at[1, last], cin.at[3, left_pad], {"az": east, "el": above}),
        ]

    def down_copies(chunk):
        if chunk == 1:
            mid = pl.ds(PAD + 64, 128)
            return [halo(5, cin.at[2, mid], cin.at[0, mid], {"az": az, "el": below})]
        one, two = pl.ds(PAD, 64), pl.ds(PAD + 192, 64)
        return [
            halo(6, cin.at[2, one], cin.at[0, one], {"az": az, "el": below}),
            halo(7, cin.at[2, two], cin.at[0, two], {"az": az, "el": below}),
            halo(8, cin.at[2, first], cin.at[0, right_pad], {"az": west, "el": below}),
            halo(9, cin.at[2, last], cin.at[0, left_pad], {"az": east, "el": below}),
        ]

    def side_copies():
        return [
            halo(10, cin.at[1, first], cin.at[1, right_pad], {"az": west, "el": el}),
            halo(11, cin.at[2, first], cin.at[2, right_pad], {"az": west, "el": el}),
            halo(12, cin.at[1, last], cin.at[1, left_pad], {"az": east, "el": el}),
            halo(13, cin.at[2, last], cin.at[2, left_pad], {"az": east, "el": el}),
        ]

    for chunk in range(2):
        span = pl.ds(chunk * HALF, HALF)
        for h in range(HEADS):
            lanes = pl.ds((h // 4) * 128, 128)
            scores = nn(kbuf[:, lanes], qmt[h, :, span]) + bias[:, span]
            top = jnp.max(scores, axis=0, keepdims=True)
            weights = jnp.exp2((scores - top).astype(BF16))
            summed = nn(vt[h], weights)
            share = summed[:HEAD, :] * (1.0 / summed[HEAD : HEAD + 1, :])
            att[pl.ds(h * HEAD, HEAD), :] = share
        attended = att[...].T.astype(BF16)
        residual = pts[span, :].astype(F32) + nn(attended, wo[...])
        normed = (residual * inv_rms(residual)).astype(BF16)
        total = residual
        for block in range(FF // D):
            cols = pl.ds(block * D, D)
            hidden = gelu(nn(normed, wh[:, cols]) + hs[span, cols]).astype(BF16)
            total = total + nn(hidden, wd[cols, :])
        conv_in = (total * inv_rms(total)).astype(BF16)
        for c, row, col, width, place in SEGMENTS:
            if c == chunk:
                joined[row, pl.ds(col, width), :] = total[place : place + width, :]
                cin[1 + row, pl.ds(PAD + col, width), :] = conv_in[place : place + width, :]

        @pl.when(el > 0)
        def _():
            for copy in up_copies(chunk):
                copy.start()

        @pl.when(el < EL - 1)
        def _():
            for copy in down_copies(chunk):
                copy.start()

        if chunk == 0:
            for copy in side_copies():
                copy.start()

    for copy in side_copies():
        copy.wait_recv()
    wc_in.wait()

    def taps(row):
        return [cin[row, pl.ds(PAD + step, COLS), :] for step in (-1, 0, 1)]

    own = jnp.concatenate(taps(1) + taps(2), axis=1)
    upper = joined[0] + nn(own, wc[pl.ds(3, 6)].reshape(6 * D, D))
    lower = joined[1] + nn(own, wc[pl.ds(0, 6)].reshape(6 * D, D))

    @pl.when(el > 0)
    def _():
        for chunk in range(2):
            for copy in down_copies(chunk):
                copy.wait_recv()

    @pl.when(el < EL - 1)
    def _():
        for chunk in range(2):
            for copy in up_copies(chunk):
                copy.wait_recv()

    upper = upper + nn(jnp.concatenate(taps(0), axis=1), wc[pl.ds(0, 3)].reshape(3 * D, D))
    lower = lower + nn(jnp.concatenate(taps(3), axis=1), wc[pl.ds(6, 3)].reshape(3 * D, D))
    out_ref[0] = upper.astype(BF16)
    out_ref[1] = lower.astype(BF16)

    for j in range(OFFSETS):
        for r in range(EL):
            if (j, r) != (REACH, 0):
                token_copy(j, r).wait_send()
    for copy in side_copies():
        copy.wait_send()

    @pl.when(el > 0)
    def _():
        for chunk in range(2):
            for copy in up_copies(chunk):
                copy.wait_send()

    @pl.when(el < EL - 1)
    def _():
        for chunk in range(2):
            for copy in down_copies(chunk):
                copy.wait_send()


def per_device(*args):
    args = args[:4] + (jnp.swapaxes(args[4], 1, 2),) + args[5:]
    any_spec = pl.BlockSpec(memory_space=pl.ANY)
    return pl.pallas_call(
        kernel,
        out_shape=jax.ShapeDtypeStruct((2, COLS, D), BF16),
        in_specs=[any_spec] * len(args),
        out_specs=pl.BlockSpec(memory_space=pltpu.VMEM),
        scratch_shapes=[
            pltpu.VMEM((POINTS, D), BF16),
            pltpu.VMEM((POINTS, D), BF16),
            pltpu.VMEM((TOK, D), BF16),
            pltpu.VMEM((OFFSETS, EL, CAP), jnp.int32),
            pltpu.VMEM((2, NEAR, COLS), jnp.int32),
            pltpu.VMEM((D, D), BF16),
            pltpu.VMEM((D, D), BF16),
            pltpu.VMEM((D, D), BF16),
            pltpu.VMEM((D, D), BF16),
            pltpu.VMEM((D, FF), BF16),
            pltpu.VMEM((D, FF), BF16),
            pltpu.VMEM((FF, D), BF16),
            pltpu.VMEM((9, D, D), BF16),
            pltpu.VMEM((SLOTS, CAP, D), BF16),
            pltpu.VMEM((SLOTS, CAP, D), BF16),
            pltpu.VMEM((HEADS, D // 2, POINTS), BF16),
            pltpu.VMEM((POINTS, FF), F32),
            pltpu.VMEM((TABLE, POINTS), F32),
            pltpu.VMEM((TABLE, D), BF16),
            pltpu.VMEM((HEADS, HEAD + 16, TABLE), BF16),
            pltpu.VMEM((D, HALF), F32),
            pltpu.VMEM((2, COLS, D), F32),
            pltpu.VMEM((4, COLS + 2 * PAD, D), BF16),
            pltpu.VMEM((D, D), BF16),
            pltpu.SemaphoreType.DMA((28,)),
            pltpu.SemaphoreType.DMA((SLOTS,)),
            pltpu.SemaphoreType.DMA((SLOTS,)),
            pltpu.SemaphoreType.DMA((14,)),
            pltpu.SemaphoreType.DMA((14,)),
        ],
        compiler_params=pltpu.CompilerParams(
            collective_id=0, has_side_effects=True, vmem_limit_bytes=56 * 1024 * 1024
        ),
        name="decoder",
    )(*args)


def solution(mesh):
    return jax.shard_map(
        per_device,
        mesh=mesh,
        in_specs=(
            P("el", "az", None),
            P("el", "az", None),
            P("az", "el", None, None),
            P("az", "el", None, None, None),
            P("el", "az", None),
            P(),
            P(),
            P(),
            P(),
            P(),
            P(),
            P(),
            P(),
        ),
        out_specs=P("el", "az", None),
        check_vma=False,
    )
```

```python
import math

import jax
import jax.numpy as jnp
from jax import lax
from jax.experimental import pallas as pl
from jax.experimental.pallas import tpu as pltpu
from jax.sharding import PartitionSpec as P

D = 256
HEADS = 8
HEAD = D // HEADS
FF = 1024
NEAR = 16
REACH = 2
OFFSETS = 5
CAP = 16
TOK = 128
COLS = 256
EL = 8
AZ = 16
SLOTS = OFFSETS * EL
POINTS = 512
HALF = 256
PAD = 16
FAR = -1e30
GELU_IN = math.sqrt(2.0 / math.pi)
GELU_CUBE = 0.044715 * GELU_IN
MESH = pl.DeviceIdType.MESH
BF16 = jnp.bfloat16
F32 = jnp.float32

RANK = (0, 1, 4, 6, 3, 7, 5, 2)
BLOCKS = 8
GROUPS = SLOTS // BLOCKS
SPAN = BLOCKS * CAP
LAG = 8
OWN = RANK[0] * OFFSETS + REACH
SEND_ORDER = (0, 1, 7, 4, 2, 6, 3, 5)

SEGMENTS = (
    (0, 0, 0, 64, 0),
    (0, 0, 192, 64, 64),
    (0, 1, 0, 64, 128),
    (0, 1, 192, 64, 192),
    (1, 0, 64, 128, 0),
    (1, 1, 64, 128, 128),
)


def nt(a, b):
    return lax.dot_general(a, b, (((1,), (1,)), ((), ())), preferred_element_type=F32)


def nn(a, b):
    return lax.dot_general(a, b, (((1,), (0,)), ((), ())), preferred_element_type=F32)


def inv_rms(x):
    return lax.rsqrt(jnp.mean(x * x, axis=-1, keepdims=True) + 1e-06)


def gelu(u):
    half = 0.5 * u
    return half + half * jnp.tanh(u * (GELU_IN + GELU_CUBE * (u * u)))


def kernel(
    points_hbm,
    skip_hbm,
    tokens_hbm,
    slots_hbm,
    index_hbm,
    wq_hbm,
    wk_hbm,
    wv_hbm,
    wo_hbm,
    wh_hbm,
    ws_hbm,
    wd_hbm,
    wc_hbm,
    out_ref,
    pts,
    skp,
    tok,
    slt,
    idx,
    wq,
    wk,
    wv,
    wo,
    wh,
    ws,
    wd,
    wc,
    payload,
    recv,
    qmt,
    hs,
    bias,
    kbuf,
    vt,
    acc,
    best,
    scores,
    att,
    joined,
    cin,
    wvt,
    in_sem,
    send_sem,
    recv_sem,
    halo_send,
    halo_recv,
):
    az = lax.axis_index("az")
    el = lax.axis_index("el")

    def az_at(step):
        return lax.rem(az + step + AZ, AZ)

    def el_at(step):
        return lax.rem(el + step, EL)

    def load(number, src, dst):
        copy = pltpu.make_async_copy(src, dst, in_sem.at[number])
        copy.start()
        return copy

    tok_in = load(0, tokens_hbm.at[0, 0], tok)
    slt_in = load(1, slots_hbm.at[0, 0], slt)

    barrier = pltpu.get_barrier_semaphore()
    for r in range(EL):
        for j in range(OFFSETS):
            if (j, r) != (REACH, 0):
                pl.semaphore_signal(
                    barrier,
                    inc=1,
                    device_id={"az": az_at(j - REACH), "el": el_at(r)},
                    device_id_type=MESH,
                )

    wq_in = load(2, wq_hbm, wq)
    pts_in = []
    skp_in = []
    for number, (chunk, row, col, width, place) in enumerate(SEGMENTS):
        here = pl.ds(chunk * HALF + place, width)
        pts_in.append(load(3 + number, points_hbm.at[row, pl.ds(col, width)], pts.at[here]))
    idx_in = load(9, index_hbm, idx)
    wv_in = load(23, wv_hbm, wv)
    wk_in = load(22, wk_hbm, wk)

    slt_in.wait()
    tok_in.wait()
    eye = (
        lax.broadcasted_iota(jnp.int32, (NEAR, NEAR), 0)
        == lax.broadcasted_iota(jnp.int32, (NEAR, NEAR), 1)
    ).astype(F32).astype(BF16)
    slot_cols = nt(eye, slt[...].reshape(SLOTS, CAP).astype(F32).astype(BF16))
    lane_id = lax.broadcasted_iota(jnp.int32, (CAP, TOK), 1).astype(F32)
    picks = jnp.concatenate(
        [
            (jnp.broadcast_to(slot_cols[:, s : s + 1], (CAP, TOK)) == lane_id)
            .astype(F32)
            .astype(BF16)
            for s in range(SLOTS)
        ],
        axis=0,
    )
    payload[...] = nn(picks, tok[...]).astype(BF16).reshape(SLOTS, CAP, D)

    pl.semaphore_wait(barrier, SLOTS - 1)

    def token_copy(j, r):
        f = el_at(r)
        place = RANK[(EL - r) % EL] * OFFSETS + j
        return pltpu.make_async_remote_copy(
            src_ref=payload.at[j * EL + f],
            dst_ref=recv.at[place],
            send_sem=send_sem.at[place],
            recv_sem=recv_sem.at[place],
            device_id={"az": az_at(j - REACH), "el": f},
            device_id_type=MESH,
        )

    for r in SEND_ORDER:
        for j in range(OFFSETS):
            if (j, r) != (REACH, 0):
                token_copy(j, r).start()
    recv[OWN] = payload[REACH * EL + el]

    for number, (chunk, row, col, width, place) in enumerate(SEGMENTS):
        here = pl.ds(chunk * HALF + place, width)
        skp_in.append(load(15 + number, skip_hbm.at[row, pl.ds(col, width)], skp.at[here]))
    ws_in = load(21, ws_hbm, ws)
    wo_in = load(24, wo_hbm, wo)
    wh_in = load(25, wh_hbm, wh)
    wd_in = load(26, wd_hbm, wd)
    wc_in = load(27, wc_hbm, wc)

    wq_in.wait()
    for copy in pts_in:
        copy.wait()
    query_t = (nt(wq[...].T, pts[...]) * (1.0 / math.sqrt(HEAD) / math.log(2.0))).astype(BF16)
    zero_rows = jnp.zeros((HEAD, POINTS), BF16)
    for h in range(HEADS):
        for part in range(4):
            rows = pl.ds(part * HEAD, HEAD)
            if part == h % 4:
                qmt[h, rows, :] = query_t[h * HEAD : (h + 1) * HEAD, :]
            else:
                qmt[h, rows, :] = zero_rows

    idx_in.wait()
    named = jnp.concatenate(
        [idx[row, :, col : col + width] for _, row, col, width, _ in SEGMENTS], axis=1
    )
    away = (lax.shift_right_logical(named, 4) - el) & (EL - 1)
    ranks = jnp.full_like(named, sum(rank << (3 * r) for r, rank in enumerate(RANK)))
    ranks = lax.shift_right_logical(ranks, away * 3) & (EL - 1)
    entries = (ranks * OFFSETS + lax.shift_right_logical(named, 7)) * CAP + (named & (CAP - 1))
    low = entries & (SPAN - 1)
    high = lax.shift_right_logical(entries, 7)
    unit = lax.shift_left(jnp.ones_like(high), high * 5)

    down = lax.broadcasted_iota(jnp.int32, (8, POINTS), 0)
    for block in range(SPAN // 8):
        total = jnp.zeros((8, POINTS), jnp.int32)
        for n in range(NEAR):
            hit = jnp.broadcast_to(low[n : n + 1, :] - block * 8, (8, POINTS)) == down
            total = total + jnp.where(hit, jnp.broadcast_to(unit[n : n + 1, :], (8, POINTS)), 0)
        for group in range(GROUPS):
            count = lax.shift_right_logical(total, 5 * group) & 31
            logs = jnp.log(count.astype(F32)) * (1.0 / math.log(2.0))
            bias[group, pl.ds(block * 8, 8), :] = jnp.where(count > 0, logs, FAR)

    wv_in.wait()
    wvt[...] = wv[...].T
    for group in range(GROUPS):
        vt[group, :, pl.ds(HEAD, 16), :] = jnp.ones((HEADS, 16, SPAN), BF16)

    @pl.when(el == 0)
    def _():
        cin[0, :, :] = jnp.zeros((COLS + 2 * PAD, D), BF16)

    @pl.when(el == EL - 1)
    def _():
        cin[3, :, :] = jnp.zeros((COLS + 2 * PAD, D), BF16)

    wk_in.wait()

    def project(group):
        for place in range(group * BLOCKS, (group + 1) * BLOCKS):
            if place != OWN:
                rank, j = divmod(place, OFFSETS)
                token_copy(j, (EL - RANK.index(rank)) % EL).wait_recv()
        rows = recv[pl.ds(group * BLOCKS, BLOCKS)].reshape(SPAN, D)
        kbuf[group] = nn(rows, wk[...]).astype(BF16)
        wide = rows.astype(F32)
        normed_tokens = (wide * inv_rms(wide)).astype(BF16)
        value_t = nt(wvt[...], normed_tokens).astype(BF16)
        for h in range(HEADS):
            vt[group, h, pl.ds(0, HEAD), :] = value_t[h * HEAD : (h + 1) * HEAD, :]

    def attend(group, chunks):
        tasks = [(chunk, h) for chunk in chunks for h in range(HEADS)]
        tops = {}
        for step in range(len(tasks) + LAG):
            if step < len(tasks):
                chunk, h = tasks[step]
                span = pl.ds(chunk * HALF, HALF)
                lanes = pl.ds((h // 4) * 128, 128)
                raw = nn(kbuf[group, :, lanes], qmt[h, :, span]) + bias[group, :, span]
                scores[step % (LAG + 1)] = raw
                top = jnp.max(raw, axis=0, keepdims=True)
                tops[step] = (top, None)
                if group > 0:
                    old = best[chunk, h][:1, :]
                    top = jnp.maximum(old, top)
                    tops[step] = (top, jnp.exp2(old - top))
                if group < GROUPS - 1:
                    best[chunk, h] = jnp.broadcast_to(top, (8, HALF))
            if step >= LAG:
                chunk, h = tasks[step - LAG]
                top, fade = tops.pop(step - LAG)
                weights = jnp.exp2((scores[(step - LAG) % (LAG + 1)] - top).astype(BF16))
                summed = nn(vt[group, h], weights)[: HEAD + 8, :]
                if group > 0:
                    summed = summed + acc[chunk, h] * fade
                acc[chunk, h] = summed

    def halo(number, src, dst, device):
        return pltpu.make_async_remote_copy(
            src_ref=src,
            dst_ref=dst,
            send_sem=halo_send.at[number],
            recv_sem=halo_recv.at[number],
            device_id=device,
            device_id_type=MESH,
        )

    west, east = az_at(-1), az_at(1)
    above = jnp.maximum(el - 1, 0)
    below = jnp.minimum(el + 1, EL - 1)
    first, last = pl.ds(PAD, PAD), pl.ds(COLS, PAD)
    left_pad, right_pad = pl.ds(0, PAD), pl.ds(PAD + COLS, PAD)

    def row_copies(chunk, row):
        number = 5 * row
        mine, theirs = (1, 3) if row == 0 else (2, 0)
        there = above if row == 0 else below
        if chunk == 1:
            mid = pl.ds(PAD + 64, 128)
            return [halo(number, cin.at[mine, mid], cin.at[theirs, mid], {"az": az, "el": there})]
        one, two = pl.ds(PAD, 64), pl.ds(PAD + 192, 64)
        return [
            halo(number + 1, cin.at[mine, one], cin.at[theirs, one], {"az": az, "el": there}),
            halo(number + 2, cin.at[mine, two], cin.at[theirs, two], {"az": az, "el": there}),
            halo(
                number + 3, cin.at[mine, first], cin.at[theirs, right_pad], {"az": west, "el": there}
            ),
            halo(
                number + 4, cin.at[mine, last], cin.at[theirs, left_pad], {"az": east, "el": there}
            ),
        ]

    def side_copies():
        return [
            halo(10, cin.at[1, first], cin.at[1, right_pad], {"az": west, "el": el}),
            halo(11, cin.at[2, first], cin.at[2, right_pad], {"az": west, "el": el}),
            halo(12, cin.at[1, last], cin.at[1, left_pad], {"az": east, "el": el}),
            halo(13, cin.at[2, last], cin.at[2, left_pad], {"az": east, "el": el}),
        ]

    def sends_row(row):
        return (el > 0) if row == 0 else (el < EL - 1)

    def join(chunk):
        for h in range(HEADS):
            share = acc[chunk, h, :HEAD, :] * (1.0 / acc[chunk, h, HEAD : HEAD + 1, :])
            att[pl.ds(h * HEAD, HEAD), :] = share.astype(BF16)
        attended = att[...].T
        for row in range(2):
            span = pl.ds(chunk * HALF + row * 128, 128)
            residual = pts[span, :].astype(F32) + nn(
                attended[row * 128 : (row + 1) * 128, :], wo[...]
            )
            normed = (residual * inv_rms(residual)).astype(BF16)
            total = residual
            for block in range(FF // D):
                cols = pl.ds(block * D, D)
                hidden = gelu(nn(normed, wh[:, cols]) + hs[span, cols]).astype(BF16)
                total = total + nn(hidden, wd[cols, :])
            conv_in = (total * inv_rms(total)).astype(BF16)
            for c, at_row, col, width, place in SEGMENTS:
                if (c, at_row) == (chunk, row):
                    start = place - row * 128
                    joined[row, pl.ds(col, width), :] = total[start : start + width, :]
                    cin[1 + row, pl.ds(PAD + col, width), :] = conv_in[start : start + width, :]

            @pl.when(sends_row(row))
            def _():
                for copy in row_copies(chunk, row):
                    copy.start()

        if chunk == 0:
            for copy in side_copies():
                copy.start()

    for group in range(2):
        project(group)
        attend(group, (0, 1))

    for copy in skp_in:
        copy.wait()
    ws_in.wait()
    for block in range(FF // D):
        cols = pl.ds(block * D, D)
        hs[:, cols] = nn(skp[...], ws[:, cols])

    for group in range(2, GROUPS - 1):
        project(group)
        attend(group, (0, 1))

    wo_in.wait()
    wh_in.wait()
    wd_in.wait()
    project(GROUPS - 1)
    for chunk in range(2):
        attend(GROUPS - 1, (chunk,))
        join(chunk)

    for copy in side_copies():
        copy.wait_recv()
    wc_in.wait()

    def taps(row):
        return [cin[row, pl.ds(PAD + step, COLS), :] for step in (-1, 0, 1)]

    own = jnp.concatenate(taps(1) + taps(2), axis=1)
    joined[0] = joined[0] + nn(own, wc[pl.ds(3, 6)].reshape(6 * D, D))
    joined[1] = joined[1] + nn(own, wc[pl.ds(0, 6)].reshape(6 * D, D))

    for j in range(OFFSETS):
        for r in range(EL):
            if (j, r) != (REACH, 0):
                token_copy(j, r).wait_send()
    for copy in side_copies():
        copy.wait_send()

    for row in range(2):

        @pl.when(sends_row(row))
        def _():
            for chunk in range(2):
                for copy in row_copies(chunk, row):
                    copy.wait_send()

    @pl.when(el > 0)
    def _():
        for chunk in range(2):
            for copy in row_copies(chunk, 1):
                copy.wait_recv()

    upper = nn(jnp.concatenate(taps(0), axis=1), wc[pl.ds(0, 3)].reshape(3 * D, D))
    out_ref[0] = (joined[0] + upper).astype(BF16)

    @pl.when(el < EL - 1)
    def _():
        for chunk in range(2):
            for copy in row_copies(chunk, 0):
                copy.wait_recv()

    lower = nn(jnp.concatenate(taps(3), axis=1), wc[pl.ds(6, 3)].reshape(3 * D, D))
    out_ref[1] = (joined[1] + lower).astype(BF16)


def per_device(*args):
    args = args[:4] + (jnp.swapaxes(args[4], 1, 2),) + args[5:]
    any_spec = pl.BlockSpec(memory_space=pl.ANY)
    return pl.pallas_call(
        kernel,
        out_shape=pltpu.VMEM((2, COLS, D), BF16),
        in_specs=[any_spec] * len(args),
        out_specs=pl.BlockSpec(memory_space=pltpu.VMEM),
        scratch_shapes=[
            pltpu.VMEM((POINTS, D), BF16),
            pltpu.VMEM((POINTS, D), BF16),
            pltpu.VMEM((TOK, D), BF16),
            pltpu.VMEM((OFFSETS, EL, CAP), jnp.int32),
            pltpu.VMEM((2, NEAR, COLS), jnp.int32),
            pltpu.VMEM((D, D), BF16),
            pltpu.VMEM((D, D), BF16),
            pltpu.VMEM((D, D), BF16),
            pltpu.VMEM((D, D), BF16),
            pltpu.VMEM((D, FF), BF16),
            pltpu.VMEM((D, FF), BF16),
            pltpu.VMEM((FF, D), BF16),
            pltpu.VMEM((9, D, D), BF16),
            pltpu.VMEM((SLOTS, CAP, D), BF16),
            pltpu.VMEM((SLOTS, CAP, D), BF16),
            pltpu.VMEM((HEADS, D // 2, POINTS), BF16),
            pltpu.VMEM((POINTS, FF), F32),
            pltpu.VMEM((GROUPS, SPAN, POINTS), F32),
            pltpu.VMEM((GROUPS, SPAN, D), BF16),
            pltpu.VMEM((GROUPS, HEADS, HEAD + 16, SPAN), BF16),
            pltpu.VMEM((2, HEADS, HEAD + 8, HALF), F32),
            pltpu.VMEM((2, HEADS, 8, HALF), F32),
            pltpu.VMEM((LAG + 1, SPAN, HALF), F32),
            pltpu.VMEM((D, HALF), BF16),
            pltpu.VMEM((2, COLS, D), F32),
            pltpu.VMEM((4, COLS + 2 * PAD, D), BF16),
            pltpu.VMEM((D, D), BF16),
            pltpu.SemaphoreType.DMA((28,)),
            pltpu.SemaphoreType.DMA((SLOTS,)),
            pltpu.SemaphoreType.DMA((SLOTS,)),
            pltpu.SemaphoreType.DMA((14,)),
            pltpu.SemaphoreType.DMA((14,)),
        ],
        compiler_params=pltpu.CompilerParams(
            collective_id=0, has_side_effects=True, vmem_limit_bytes=56 * 1024 * 1024
        ),
        name="decoder",
    )(*args)


def solution(mesh):
    return jax.shard_map(
        per_device,
        mesh=mesh,
        in_specs=(
            P("el", "az", None),
            P("el", "az", None),
            P("az", "el", None, None),
            P("az", "el", None, None, None),
            P("el", "az", None),
            P(),
            P(),
            P(),
            P(),
            P(),
            P(),
            P(),
            P(),
        ),
        out_specs=P("el", "az", None),
        check_vma=False,
    )
```

```python
import math

import jax
import jax.numpy as jnp
from jax import lax
from jax.experimental import pallas as pl
from jax.experimental.pallas import tpu as pltpu
from jax.sharding import PartitionSpec as P

D = 256
HEADS = 8
HEAD = D // HEADS
FF = 1024
NEAR = 16
REACH = 2
OFFSETS = 5
CAP = 16
TOK = 128
COLS = 256
EL = 8
AZ = 16
SLOTS = OFFSETS * EL
POINTS = 512
HALF = 256
PAD = 16
FAR = -1e30
GELU_IN = math.sqrt(2.0 / math.pi)
GELU_CUBE = 0.044715 * GELU_IN
MESH = pl.DeviceIdType.MESH
BF16 = jnp.bfloat16
F32 = jnp.float32

RANK = (0, 1, 4, 6, 3, 7, 5, 2)
BLOCKS = 8
GROUPS = SLOTS // BLOCKS
SPAN = BLOCKS * CAP
LAG = 8
SKIP_GROUP = 1
OWN = RANK[0] * OFFSETS + REACH
SEND_ORDER = (0, 1, 7, 4, 2, 6, 3, 5)

SEGMENTS = (
    (0, 0, 0, 64, 0),
    (0, 0, 192, 64, 64),
    (0, 1, 0, 64, 128),
    (0, 1, 192, 64, 192),
    (1, 0, 64, 128, 0),
    (1, 1, 64, 128, 128),
)


def nt(a, b):
    return lax.dot_general(a, b, (((1,), (1,)), ((), ())), preferred_element_type=F32)


def nn(a, b):
    return lax.dot_general(a, b, (((1,), (0,)), ((), ())), preferred_element_type=F32)


def inv_rms(x):
    return lax.rsqrt(jnp.mean(x * x, axis=-1, keepdims=True) + 1e-06)


def gelu(u):
    half = BF16(0.5) * u
    return half + half * jnp.tanh(u * (BF16(GELU_IN) + BF16(GELU_CUBE) * (u * u)))


def kernel(
    points_hbm,
    skip_hbm,
    tokens_hbm,
    slots_hbm,
    index_hbm,
    wq_hbm,
    wk_hbm,
    wv_hbm,
    wo_hbm,
    wh_hbm,
    ws_hbm,
    wd_hbm,
    wc_hbm,
    out_ref,
    pts,
    skp,
    tok,
    slt,
    idx,
    wq,
    wk,
    wv,
    wo,
    wh,
    ws,
    wd,
    wc,
    payload,
    recv,
    qmt,
    hs,
    bias,
    kbuf,
    vt,
    acc,
    best,
    scores,
    att,
    joined,
    cin,
    wvt,
    in_sem,
    send_sem,
    recv_sem,
    halo_send,
    halo_recv,
):
    az = lax.axis_index("az")
    el = lax.axis_index("el")

    def az_at(step):
        return lax.rem(az + step + AZ, AZ)

    def el_at(step):
        return lax.rem(el + step, EL)

    def load(number, src, dst):
        copy = pltpu.make_async_copy(src, dst, in_sem.at[number])
        copy.start()
        return copy

    tok_in = load(0, tokens_hbm.at[0, 0], tok)
    slt_in = load(1, slots_hbm.at[0, 0], slt)

    barrier = pltpu.get_barrier_semaphore()
    for r in range(EL):
        for j in range(OFFSETS):
            if (j, r) != (REACH, 0):
                pl.semaphore_signal(
                    barrier,
                    inc=1,
                    device_id={"az": az_at(j - REACH), "el": el_at(r)},
                    device_id_type=MESH,
                )

    wq_in = load(2, wq_hbm, wq)
    pts_in = []
    skp_in = []
    for number, (chunk, row, col, width, place) in enumerate(SEGMENTS):
        here = pl.ds(chunk * HALF + place, width)
        pts_in.append(load(3 + number, points_hbm.at[row, pl.ds(col, width)], pts.at[here]))
    idx_in = load(9, index_hbm, idx)
    wv_in = load(23, wv_hbm, wv)
    wk_in = load(22, wk_hbm, wk)

    slt_in.wait()
    tok_in.wait()
    eye = (
        lax.broadcasted_iota(jnp.int32, (NEAR, NEAR), 0)
        == lax.broadcasted_iota(jnp.int32, (NEAR, NEAR), 1)
    ).astype(F32).astype(BF16)
    slot_cols = nt(eye, slt[...].reshape(SLOTS, CAP).astype(F32).astype(BF16))
    lane_id = lax.broadcasted_iota(jnp.int32, (CAP, TOK), 1).astype(F32)
    picks = jnp.concatenate(
        [
            (jnp.broadcast_to(slot_cols[:, s : s + 1], (CAP, TOK)) == lane_id)
            .astype(F32)
            .astype(BF16)
            for s in range(SLOTS)
        ],
        axis=0,
    )
    payload[...] = nn(picks, tok[...]).astype(BF16).reshape(SLOTS, CAP, D)

    pl.semaphore_wait(barrier, SLOTS - 1)

    def token_copy(j, r):
        f = el_at(r)
        place = RANK[(EL - r) % EL] * OFFSETS + j
        return pltpu.make_async_remote_copy(
            src_ref=payload.at[j * EL + f],
            dst_ref=recv.at[place],
            send_sem=send_sem.at[place],
            recv_sem=recv_sem.at[place],
            device_id={"az": az_at(j - REACH), "el": f},
            device_id_type=MESH,
        )

    for r in SEND_ORDER:
        for j in range(OFFSETS):
            if (j, r) != (REACH, 0):
                token_copy(j, r).start()
    recv[OWN] = payload[REACH * EL + el]

    for number, (chunk, row, col, width, place) in enumerate(SEGMENTS):
        here = pl.ds(chunk * HALF + place, width)
        skp_in.append(load(15 + number, skip_hbm.at[row, pl.ds(col, width)], skp.at[here]))
    ws_in = load(21, ws_hbm, ws)
    wo_in = load(24, wo_hbm, wo)
    wh_in = load(25, wh_hbm, wh)
    wd_in = load(26, wd_hbm, wd)
    wc_in = load(27, wc_hbm, wc)

    wq_in.wait()
    for copy in pts_in:
        copy.wait()
    query_t = (nt(wq[...].T, pts[...]) * (1.0 / math.sqrt(HEAD) / math.log(2.0))).astype(BF16)
    zero_rows = jnp.zeros((HEAD, POINTS), BF16)
    for h in range(HEADS):
        for part in range(4):
            rows = pl.ds(part * HEAD, HEAD)
            if part == h % 4:
                qmt[h, rows, :] = query_t[h * HEAD : (h + 1) * HEAD, :]
            else:
                qmt[h, rows, :] = zero_rows

    idx_in.wait()
    named = jnp.concatenate(
        [idx[row, :, col : col + width] for _, row, col, width, _ in SEGMENTS], axis=1
    )
    away = (lax.shift_right_logical(named, 4) - el) & (EL - 1)
    ranks = jnp.full_like(named, sum(rank << (3 * r) for r, rank in enumerate(RANK)))
    ranks = lax.shift_right_logical(ranks, away * 3) & (EL - 1)
    entries = (ranks * OFFSETS + lax.shift_right_logical(named, 7)) * CAP + (named & (CAP - 1))
    low = entries & (SPAN - 1)
    high = lax.shift_right_logical(entries, 7)
    unit = lax.shift_left(jnp.ones_like(high), high * 5)

    down = lax.broadcasted_iota(jnp.int32, (8, POINTS), 0)
    for block in range(SPAN // 8):
        total = jnp.zeros((8, POINTS), jnp.int32)
        for n in range(NEAR):
            hit = jnp.broadcast_to(low[n : n + 1, :] - block * 8, (8, POINTS)) == down
            total = total + jnp.where(hit, jnp.broadcast_to(unit[n : n + 1, :], (8, POINTS)), 0)
        for group in range(GROUPS):
            count = lax.shift_right_logical(total, 5 * group) & 31
            bias[group, pl.ds(block * 8, 8), :] = jnp.maximum(jnp.log2(count.astype(F32)), FAR)

    wv_in.wait()
    wvt[...] = wv[...].T
    for group in range(GROUPS):
        vt[group, :, pl.ds(HEAD, 16), :] = jnp.ones((HEADS, 16, SPAN), BF16)

    @pl.when(el == 0)
    def _():
        cin[0, :, :] = jnp.zeros((COLS + 2 * PAD, D), BF16)

    @pl.when(el == EL - 1)
    def _():
        cin[3, :, :] = jnp.zeros((COLS + 2 * PAD, D), BF16)

    wk_in.wait()

    def project(group):
        for place in range(group * BLOCKS, (group + 1) * BLOCKS):
            if place != OWN:
                rank, j = divmod(place, OFFSETS)
                token_copy(j, (EL - RANK.index(rank)) % EL).wait_recv()
        rows = recv[pl.ds(group * BLOCKS, BLOCKS)].reshape(SPAN, D)
        kbuf[group] = nn(rows, wk[...]).astype(BF16)
        wide = rows.astype(F32)
        normed_tokens = (wide * inv_rms(wide)).astype(BF16)
        value_t = nt(wvt[...], normed_tokens).astype(BF16)
        for h in range(HEADS):
            vt[group, h, pl.ds(0, HEAD), :] = value_t[h * HEAD : (h + 1) * HEAD, :]

    pending = []
    begun = [0]

    def begin(group, chunk, h):
        span = pl.ds(chunk * HALF, HALF)
        lanes = pl.ds((h // 4) * 128, 128)
        slot = begun[0] % (LAG + 1)
        begun[0] += 1
        raw = nn(kbuf[group, :, lanes], qmt[h, :, span]) + bias[group, :, span]
        scores[slot] = raw
        top = jnp.max(raw, axis=0, keepdims=True)
        fade = None
        if group > 0:
            old = best[chunk, h][:1, :]
            top = jnp.maximum(old, top)
            fade = jnp.exp2(old - top)
        if group < GROUPS - 1:
            best[chunk, h] = jnp.broadcast_to(top, (8, HALF))
        pending.append((group, chunk, h, slot, top, fade))

    def finish():
        group, chunk, h, slot, top, fade = pending.pop(0)
        weights = jnp.exp2((scores[slot] - top).astype(BF16))
        summed = nn(vt[group, h], weights)[: HEAD + 8, :]
        if group > 0:
            summed = summed + acc[chunk, h] * fade
        acc[chunk, h] = summed

    def halo(number, src, dst, device):
        return pltpu.make_async_remote_copy(
            src_ref=src,
            dst_ref=dst,
            send_sem=halo_send.at[number],
            recv_sem=halo_recv.at[number],
            device_id=device,
            device_id_type=MESH,
        )

    west, east = az_at(-1), az_at(1)
    above = jnp.maximum(el - 1, 0)
    below = jnp.minimum(el + 1, EL - 1)
    first, last = pl.ds(PAD, PAD), pl.ds(COLS, PAD)
    left_pad, right_pad = pl.ds(0, PAD), pl.ds(PAD + COLS, PAD)

    def row_copies(chunk, row):
        number = 5 * row
        mine, theirs = (1, 3) if row == 0 else (2, 0)
        there = above if row == 0 else below
        if chunk == 1:
            mid = pl.ds(PAD + 64, 128)
            return [halo(number, cin.at[mine, mid], cin.at[theirs, mid], {"az": az, "el": there})]
        one, two = pl.ds(PAD, 64), pl.ds(PAD + 192, 64)
        return [
            halo(number + 1, cin.at[mine, one], cin.at[theirs, one], {"az": az, "el": there}),
            halo(number + 2, cin.at[mine, two], cin.at[theirs, two], {"az": az, "el": there}),
            halo(
                number + 3, cin.at[mine, first], cin.at[theirs, right_pad], {"az": west, "el": there}
            ),
            halo(
                number + 4, cin.at[mine, last], cin.at[theirs, left_pad], {"az": east, "el": there}
            ),
        ]

    def side_copies():
        return [
            halo(10, cin.at[1, first], cin.at[1, right_pad], {"az": west, "el": el}),
            halo(11, cin.at[2, first], cin.at[2, right_pad], {"az": west, "el": el}),
            halo(12, cin.at[1, last], cin.at[1, left_pad], {"az": east, "el": el}),
            halo(13, cin.at[2, last], cin.at[2, left_pad], {"az": east, "el": el}),
        ]

    def sends_row(row):
        return (el > 0) if row == 0 else (el < EL - 1)

    def join(chunk):
        for h in range(HEADS):
            share = acc[chunk, h, :HEAD, :] * (1.0 / acc[chunk, h, HEAD : HEAD + 1, :])
            att[pl.ds(h * HEAD, HEAD), :] = share.astype(BF16)
        attended = att[...].T
        for row in (1, 0):
            span = pl.ds(chunk * HALF + row * 128, 128)
            residual = pts[span, :].astype(F32) + nn(
                attended[row * 128 : (row + 1) * 128, :], wo[...]
            )
            normed = (residual * inv_rms(residual)).astype(BF16)
            total = residual
            for block in range(FF // D):
                cols = pl.ds(block * D, D)
                hidden = gelu((nn(normed, wh[:, cols]) + hs[span, cols]).astype(BF16))
                total = total + nn(hidden, wd[cols, :])
            conv_in = (total * inv_rms(total)).astype(BF16)
            for c, at_row, col, width, place in SEGMENTS:
                if (c, at_row) == (chunk, row):
                    start = place - row * 128
                    joined[row, pl.ds(col, width), :] = total[start : start + width, :]
                    cin[1 + row, pl.ds(PAD + col, width), :] = conv_in[start : start + width, :]

            for _ in range(min(HEADS // 2, len(pending))):
                finish()

            @pl.when(sends_row(row))
            def _():
                for copy in row_copies(chunk, row):
                    copy.start()

        if chunk == 0:
            for copy in side_copies():
                copy.start()

    def skip_part(block):
        cols = pl.ds(block * D, D)
        hs[:, cols] = nn(skp[...], ws[:, cols])

    for group in range(GROUPS - 1):
        project(group)
        if group == SKIP_GROUP:
            for copy in skp_in:
                copy.wait()
            ws_in.wait()
        for chunk in range(2):
            for h in range(HEADS):
                begin(group, chunk, h)
                if len(pending) > LAG:
                    finish()
                if group == SKIP_GROUP and h % 4 == 3:
                    skip_part(2 * chunk + h // 4)
    while pending:
        finish()

    wo_in.wait()
    wh_in.wait()
    wd_in.wait()
    project(GROUPS - 1)
    for chunk in range(2):
        for h in range(HEADS):
            begin(GROUPS - 1, chunk, h)
            if chunk == 1:
                finish()
    join(0)
    join(1)

    for copy in side_copies():
        copy.wait_recv()
    wc_in.wait()

    def taps(row):
        return [cin[row, pl.ds(PAD + step, COLS), :] for step in (-1, 0, 1)]

    own = jnp.concatenate(taps(1) + taps(2), axis=1)
    joined[0] = joined[0] + nn(own, wc[pl.ds(3, 6)].reshape(6 * D, D))
    joined[1] = joined[1] + nn(own, wc[pl.ds(0, 6)].reshape(6 * D, D))

    for j in range(OFFSETS):
        for r in range(EL):
            if (j, r) != (REACH, 0):
                token_copy(j, r).wait_send()
    for copy in side_copies():
        copy.wait_send()

    for row in range(2):

        @pl.when(sends_row(row))
        def _():
            for chunk in range(2):
                for copy in row_copies(chunk, row):
                    copy.wait_send()

    @pl.when(el > 0)
    def _():
        for chunk in range(2):
            for copy in row_copies(chunk, 1):
                copy.wait_recv()

    upper = nn(jnp.concatenate(taps(0), axis=1), wc[pl.ds(0, 3)].reshape(3 * D, D))
    out_ref[0] = (joined[0] + upper).astype(BF16)

    @pl.when(el < EL - 1)
    def _():
        for chunk in range(2):
            for copy in row_copies(chunk, 0):
                copy.wait_recv()

    lower = nn(jnp.concatenate(taps(3), axis=1), wc[pl.ds(6, 3)].reshape(3 * D, D))
    out_ref[1] = (joined[1] + lower).astype(BF16)


def per_device(*args):
    args = args[:4] + (jnp.swapaxes(args[4], 1, 2),) + args[5:]
    any_spec = pl.BlockSpec(memory_space=pl.ANY)
    return pl.pallas_call(
        kernel,
        out_shape=pltpu.VMEM((2, COLS, D), BF16),
        in_specs=[any_spec] * len(args),
        out_specs=pl.BlockSpec(memory_space=pltpu.VMEM),
        scratch_shapes=[
            pltpu.VMEM((POINTS, D), BF16),
            pltpu.VMEM((POINTS, D), BF16),
            pltpu.VMEM((TOK, D), BF16),
            pltpu.VMEM((OFFSETS, EL, CAP), jnp.int32),
            pltpu.VMEM((2, NEAR, COLS), jnp.int32),
            pltpu.VMEM((D, D), BF16),
            pltpu.VMEM((D, D), BF16),
            pltpu.VMEM((D, D), BF16),
            pltpu.VMEM((D, D), BF16),
            pltpu.VMEM((D, FF), BF16),
            pltpu.VMEM((D, FF), BF16),
            pltpu.VMEM((FF, D), BF16),
            pltpu.VMEM((9, D, D), BF16),
            pltpu.VMEM((SLOTS, CAP, D), BF16),
            pltpu.VMEM((SLOTS, CAP, D), BF16),
            pltpu.VMEM((HEADS, D // 2, POINTS), BF16),
            pltpu.VMEM((POINTS, FF), F32),
            pltpu.VMEM((GROUPS, SPAN, POINTS), F32),
            pltpu.VMEM((GROUPS, SPAN, D), BF16),
            pltpu.VMEM((GROUPS, HEADS, HEAD + 16, SPAN), BF16),
            pltpu.VMEM((2, HEADS, HEAD + 8, HALF), F32),
            pltpu.VMEM((2, HEADS, 8, HALF), F32),
            pltpu.VMEM((LAG + 1, SPAN, HALF), F32),
            pltpu.VMEM((D, HALF), BF16),
            pltpu.VMEM((2, COLS, D), F32),
            pltpu.VMEM((4, COLS + 2 * PAD, D), BF16),
            pltpu.VMEM((D, D), BF16),
            pltpu.SemaphoreType.DMA((28,)),
            pltpu.SemaphoreType.DMA((SLOTS,)),
            pltpu.SemaphoreType.DMA((SLOTS,)),
            pltpu.SemaphoreType.DMA((14,)),
            pltpu.SemaphoreType.DMA((14,)),
        ],
        compiler_params=pltpu.CompilerParams(
            collective_id=0, has_side_effects=True, vmem_limit_bytes=56 * 1024 * 1024
        ),
        name="decoder",
    )(*args)


def solution(mesh):
    return jax.shard_map(
        per_device,
        mesh=mesh,
        in_specs=(
            P("el", "az", None),
            P("el", "az", None),
            P("az", "el", None, None),
            P("az", "el", None, None, None),
            P("el", "az", None),
            P(),
            P(),
            P(),
            P(),
            P(),
            P(),
            P(),
            P(),
        ),
        out_specs=P("el", "az", None),
        check_vma=False,
    )
```

```python
import math

import jax
import jax.numpy as jnp
from jax import lax
from jax.experimental import pallas as pl
from jax.experimental.pallas import tpu as pltpu
from jax.sharding import PartitionSpec as P

D = 256
HEADS = 8
HEAD = D // HEADS
FF = 1024
NEAR = 16
REACH = 2
OFFSETS = 5
CAP = 16
TOK = 128
COLS = 256
EL = 8
AZ = 16
SLOTS = OFFSETS * EL
POINTS = 512
HALF = 256
PAD = 16
FAR = -1e30
GELU_IN = math.sqrt(2.0 / math.pi)
GELU_CUBE = 0.044715 * GELU_IN
MESH = pl.DeviceIdType.MESH
BF16 = jnp.bfloat16
F32 = jnp.float32

SPAN = EL * CAP
ORDER = (2, 1, 3, 0, 4)
FAR_FIRST = (2, 6, 3, 5, 4, 1, 7)
LAG = 8
SKIP_GROUP = 1
OWN = REACH * EL

SEGMENTS = (
    (0, 0, 0, 64, 0),
    (0, 0, 192, 64, 64),
    (0, 1, 0, 64, 128),
    (0, 1, 192, 64, 192),
    (1, 0, 64, 128, 0),
    (1, 1, 64, 128, 128),
)


def nt(a, b):
    return lax.dot_general(a, b, (((1,), (1,)), ((), ())), preferred_element_type=F32)


def nn(a, b):
    return lax.dot_general(a, b, (((1,), (0,)), ((), ())), preferred_element_type=F32)


def inv_rms(x):
    return lax.rsqrt(jnp.mean(x * x, axis=-1, keepdims=True) + 1e-06)


def gelu(u):
    half = BF16(0.5) * u
    return half + half * jnp.tanh(u * (BF16(GELU_IN) + BF16(GELU_CUBE) * (u * u)))


def kernel(
    points_hbm,
    skip_hbm,
    tokens_hbm,
    slots_hbm,
    index_hbm,
    wq_hbm,
    wk_hbm,
    wv_hbm,
    wo_hbm,
    wh_hbm,
    ws_hbm,
    wd_hbm,
    wc_hbm,
    out_ref,
    pts,
    skp,
    tok,
    slt,
    idx,
    wq,
    wk,
    wv,
    wo,
    wh,
    ws,
    wd,
    wc,
    payload,
    recv,
    qmt,
    hs,
    bias,
    kbuf,
    vt,
    acc,
    best,
    scores,
    att,
    joined,
    cin,
    wvt,
    in_sem,
    send_sem,
    recv_sem,
    ready,
    halo_send,
    halo_recv,
):
    az = lax.axis_index("az")
    el = lax.axis_index("el")

    def az_at(step):
        return lax.rem(az + step + AZ, AZ)

    def el_at(step):
        return lax.rem(el + step, EL)

    def load(number, src, dst):
        copy = pltpu.make_async_copy(src, dst, in_sem.at[number])
        copy.start()
        return copy

    tok_in = load(0, tokens_hbm.at[0, 0], tok)
    slt_in = load(1, slots_hbm.at[0, 0], slt)

    near = [(REACH, r) for r in range(1, EL)] + [(j, 0) for j in range(OFFSETS) if j != REACH]
    barrier = pltpu.get_barrier_semaphore()
    for j, r in near:
        pl.semaphore_signal(
            barrier,
            inc=1,
            device_id={"az": az_at(j - REACH), "el": el_at(r)},
            device_id_type=MESH,
        )

    wq_in = load(2, wq_hbm, wq)
    pts_in = []
    skp_in = []
    for number, (chunk, row, col, width, place) in enumerate(SEGMENTS):
        here = pl.ds(chunk * HALF + place, width)
        pts_in.append(load(3 + number, points_hbm.at[row, pl.ds(col, width)], pts.at[here]))
    idx_in = load(9, index_hbm, idx)
    wv_in = load(23, wv_hbm, wv)
    wk_in = load(22, wk_hbm, wk)

    slt_in.wait()
    tok_in.wait()
    eye = (
        lax.broadcasted_iota(jnp.int32, (NEAR, NEAR), 0)
        == lax.broadcasted_iota(jnp.int32, (NEAR, NEAR), 1)
    ).astype(F32).astype(BF16)
    slot_cols = nt(eye, slt[...].reshape(SLOTS, CAP).astype(F32).astype(BF16))
    lane_id = lax.broadcasted_iota(jnp.int32, (CAP, TOK), 1).astype(F32)
    picks = jnp.concatenate(
        [
            (jnp.broadcast_to(slot_cols[:, s : s + 1], (CAP, TOK)) == lane_id)
            .astype(F32)
            .astype(BF16)
            for s in range(SLOTS)
        ],
        axis=0,
    )
    payload[...] = nn(picks, tok[...]).astype(BF16).reshape(SLOTS, CAP, D)

    def token_copy(j, r):
        f = el_at(r)
        place = j * EL + (EL - r) % EL
        return pltpu.make_async_remote_copy(
            src_ref=payload.at[j * EL + f],
            dst_ref=recv.at[place],
            send_sem=send_sem.at[place],
            recv_sem=recv_sem.at[place],
            device_id={"az": az_at(j - REACH), "el": f},
            device_id_type=MESH,
        )

    def send_block(j):
        pl.semaphore_wait(ready.at[OFFSETS - 1 - j], 1)
        for r in FAR_FIRST:
            token_copy(j, r).start()

    pl.semaphore_wait(barrier, len(near))
    for j in range(OFFSETS):
        if j != REACH:
            pl.semaphore_signal(
                ready.at[j],
                inc=1,
                device_id={"az": az_at(j - REACH), "el": el},
                device_id_type=MESH,
            )
    for r in FAR_FIRST:
        token_copy(REACH, r).start()
    for j in (3, 4, 1, 0):
        token_copy(j, 0).start()
    send_block(3)
    send_block(4)
    recv[OWN] = payload[REACH * EL + el]

    for number, (chunk, row, col, width, place) in enumerate(SEGMENTS):
        here = pl.ds(chunk * HALF + place, width)
        skp_in.append(load(15 + number, skip_hbm.at[row, pl.ds(col, width)], skp.at[here]))
    ws_in = load(21, ws_hbm, ws)
    wo_in = load(24, wo_hbm, wo)
    wh_in = load(25, wh_hbm, wh)
    wd_in = load(26, wd_hbm, wd)
    wc_in = load(27, wc_hbm, wc)

    wq_in.wait()
    for copy in pts_in:
        copy.wait()
    query_t = (nt(wq[...].T, pts[...]) * (1.0 / math.sqrt(HEAD) / math.log(2.0))).astype(BF16)
    zero_rows = jnp.zeros((HEAD, POINTS), BF16)
    for h in range(HEADS):
        for part in range(4):
            rows = pl.ds(part * HEAD, HEAD)
            if part == h % 4:
                qmt[h, rows, :] = query_t[h * HEAD : (h + 1) * HEAD, :]
            else:
                qmt[h, rows, :] = zero_rows

    idx_in.wait()
    named = jnp.concatenate(
        [idx[row, :, col : col + width] for _, row, col, width, _ in SEGMENTS], axis=1
    )
    away = (lax.shift_right_logical(named, 4) - el) & (EL - 1)
    entries = (named & ~(SPAN - 1)) + away * CAP + (named & (CAP - 1))
    low = entries & (SPAN - 1)
    high = lax.shift_right_logical(entries, 7)
    unit = lax.shift_left(jnp.ones_like(high), high * 5)

    down = lax.broadcasted_iota(jnp.int32, (8, POINTS), 0)
    for block in range(SPAN // 8):
        total = jnp.zeros((8, POINTS), jnp.int32)
        for n in range(NEAR):
            hit = jnp.broadcast_to(low[n : n + 1, :] - block * 8, (8, POINTS)) == down
            total = total + jnp.where(hit, jnp.broadcast_to(unit[n : n + 1, :], (8, POINTS)), 0)
        for group in range(OFFSETS):
            count = lax.shift_right_logical(total, 5 * group) & 31
            bias[group, pl.ds(block * 8, 8), :] = jnp.maximum(jnp.log2(count.astype(F32)), FAR)

    send_block(1)
    send_block(0)

    wv_in.wait()
    wvt[...] = wv[...].T
    for group in range(OFFSETS):
        vt[group, :, pl.ds(HEAD, 16), :] = jnp.ones((HEADS, 16, SPAN), BF16)

    @pl.when(el == 0)
    def _():
        cin[0, :, :] = jnp.zeros((COLS + 2 * PAD, D), BF16)

    @pl.when(el == EL - 1)
    def _():
        cin[3, :, :] = jnp.zeros((COLS + 2 * PAD, D), BF16)

    wk_in.wait()

    def project(group):
        for place in range(EL):
            if group * EL + place != OWN:
                token_copy(group, (EL - place) % EL).wait_recv()
        rows = recv[pl.ds(group * EL, EL)].reshape(SPAN, D)
        kbuf[group] = nn(rows, wk[...]).astype(BF16)
        wide = rows.astype(F32)
        normed_tokens = (wide * inv_rms(wide)).astype(BF16)
        value_t = nt(wvt[...], normed_tokens).astype(BF16)
        for h in range(HEADS):
            vt[group, h, pl.ds(0, HEAD), :] = value_t[h * HEAD : (h + 1) * HEAD, :]

    pending = []
    begun = [0]

    def begin(group, chunk, h):
        span = pl.ds(chunk * HALF, HALF)
        lanes = pl.ds((h // 4) * 128, 128)
        slot = begun[0] % (LAG + 1)
        begun[0] += 1
        raw = nn(kbuf[group, :, lanes], qmt[h, :, span]) + bias[group, :, span]
        scores[slot] = raw
        top = jnp.max(raw, axis=0, keepdims=True)
        fade = None
        if group != ORDER[0]:
            old = best[chunk, h][:1, :]
            top = jnp.maximum(old, top)
            fade = jnp.exp2(old - top)
        if group != ORDER[-1]:
            best[chunk, h] = jnp.broadcast_to(top, (8, HALF))
        pending.append((group, chunk, h, slot, top, fade))

    def finish():
        group, chunk, h, slot, top, fade = pending.pop(0)
        weights = jnp.exp2((scores[slot] - top).astype(BF16))
        summed = nn(vt[group, h], weights)[: HEAD + 8, :]
        if group != ORDER[0]:
            summed = summed + acc[chunk, h] * fade
        acc[chunk, h] = summed

    def halo(number, src, dst, device):
        return pltpu.make_async_remote_copy(
            src_ref=src,
            dst_ref=dst,
            send_sem=halo_send.at[number],
            recv_sem=halo_recv.at[number],
            device_id=device,
            device_id_type=MESH,
        )

    west, east = az_at(-1), az_at(1)
    above = jnp.maximum(el - 1, 0)
    below = jnp.minimum(el + 1, EL - 1)
    first, last = pl.ds(PAD, PAD), pl.ds(COLS, PAD)
    left_pad, right_pad = pl.ds(0, PAD), pl.ds(PAD + COLS, PAD)

    def row_copies(chunk, row):
        number = 5 * row
        mine, theirs = (1, 3) if row == 0 else (2, 0)
        there = above if row == 0 else below
        if chunk == 1:
            mid = pl.ds(PAD + 64, 128)
            return [halo(number, cin.at[mine, mid], cin.at[theirs, mid], {"az": az, "el": there})]
        one, two = pl.ds(PAD, 64), pl.ds(PAD + 192, 64)
        return [
            halo(number + 1, cin.at[mine, one], cin.at[theirs, one], {"az": az, "el": there}),
            halo(number + 2, cin.at[mine, two], cin.at[theirs, two], {"az": az, "el": there}),
            halo(
                number + 3, cin.at[mine, first], cin.at[theirs, right_pad], {"az": west, "el": there}
            ),
            halo(
                number + 4, cin.at[mine, last], cin.at[theirs, left_pad], {"az": east, "el": there}
            ),
        ]

    def side_copies():
        return [
            halo(10, cin.at[1, first], cin.at[1, right_pad], {"az": west, "el": el}),
            halo(11, cin.at[2, first], cin.at[2, right_pad], {"az": west, "el": el}),
            halo(12, cin.at[1, last], cin.at[1, left_pad], {"az": east, "el": el}),
            halo(13, cin.at[2, last], cin.at[2, left_pad], {"az": east, "el": el}),
        ]

    def sends_row(row):
        return (el > 0) if row == 0 else (el < EL - 1)

    def join(chunk):
        for h in range(HEADS):
            share = acc[chunk, h, :HEAD, :] * (1.0 / acc[chunk, h, HEAD : HEAD + 1, :])
            att[pl.ds(h * HEAD, HEAD), :] = share.astype(BF16)
        attended = att[...].T
        for row in (1, 0):
            span = pl.ds(chunk * HALF + row * 128, 128)
            residual = pts[span, :].astype(F32) + nn(
                attended[row * 128 : (row + 1) * 128, :], wo[...]
            )
            normed = (residual * inv_rms(residual)).astype(BF16)
            total = residual
            for block in range(FF // D):
                cols = pl.ds(block * D, D)
                hidden = gelu((nn(normed, wh[:, cols]) + hs[span, cols]).astype(BF16))
                total = total + nn(hidden, wd[cols, :])
            conv_in = (total * inv_rms(total)).astype(BF16)
            for c, at_row, col, width, place in SEGMENTS:
                if (c, at_row) == (chunk, row):
                    start = place - row * 128
                    joined[row, pl.ds(col, width), :] = total[start : start + width, :]
                    cin[1 + row, pl.ds(PAD + col, width), :] = conv_in[start : start + width, :]

            for _ in range(min(HEADS // 2, len(pending))):
                finish()

            @pl.when(sends_row(row))
            def _():
                for copy in row_copies(chunk, row):
                    copy.start()

        if chunk == 0:
            for copy in side_copies():
                copy.start()

    def skip_part(block):
        cols = pl.ds(block * D, D)
        hs[:, cols] = nn(skp[...], ws[:, cols])

    for group in ORDER[:-1]:
        project(group)
        if group == SKIP_GROUP:
            for copy in skp_in:
                copy.wait()
            ws_in.wait()
        for chunk in range(2):
            for h in range(HEADS):
                begin(group, chunk, h)
                if len(pending) > LAG:
                    finish()
                if group == SKIP_GROUP and h % 4 == 3:
                    skip_part(2 * chunk + h // 4)
    while pending:
        finish()

    wo_in.wait()
    wh_in.wait()
    wd_in.wait()
    project(ORDER[-1])
    for chunk in range(2):
        for h in range(HEADS):
            begin(ORDER[-1], chunk, h)
            if chunk == 1:
                finish()
    join(0)
    join(1)

    for copy in side_copies():
        copy.wait_recv()
    wc_in.wait()

    def taps(row):
        return [cin[row, pl.ds(PAD + step, COLS), :] for step in (-1, 0, 1)]

    own = jnp.concatenate(taps(1) + taps(2), axis=1)
    joined[0] = joined[0] + nn(own, wc[pl.ds(3, 6)].reshape(6 * D, D))
    joined[1] = joined[1] + nn(own, wc[pl.ds(0, 6)].reshape(6 * D, D))

    for j in range(OFFSETS):
        for r in range(EL):
            if (j, r) != (REACH, 0):
                token_copy(j, r).wait_send()
    for copy in side_copies():
        copy.wait_send()

    for row in range(2):

        @pl.when(sends_row(row))
        def _():
            for chunk in range(2):
                for copy in row_copies(chunk, row):
                    copy.wait_send()

    @pl.when(el > 0)
    def _():
        for chunk in range(2):
            for copy in row_copies(chunk, 1):
                copy.wait_recv()

    upper = nn(jnp.concatenate(taps(0), axis=1), wc[pl.ds(0, 3)].reshape(3 * D, D))
    out_ref[0] = (joined[0] + upper).astype(BF16)

    @pl.when(el < EL - 1)
    def _():
        for chunk in range(2):
            for copy in row_copies(chunk, 0):
                copy.wait_recv()

    lower = nn(jnp.concatenate(taps(3), axis=1), wc[pl.ds(6, 3)].reshape(3 * D, D))
    out_ref[1] = (joined[1] + lower).astype(BF16)


def per_device(*args):
    args = args[:4] + (jnp.swapaxes(args[4], 1, 2),) + args[5:]
    any_spec = pl.BlockSpec(memory_space=pl.ANY)
    return pl.pallas_call(
        kernel,
        out_shape=pltpu.VMEM((2, COLS, D), BF16),
        in_specs=[any_spec] * len(args),
        out_specs=pl.BlockSpec(memory_space=pltpu.VMEM),
        scratch_shapes=[
            pltpu.VMEM((POINTS, D), BF16),
            pltpu.VMEM((POINTS, D), BF16),
            pltpu.VMEM((TOK, D), BF16),
            pltpu.VMEM((OFFSETS, EL, CAP), jnp.int32),
            pltpu.VMEM((2, NEAR, COLS), jnp.int32),
            pltpu.VMEM((D, D), BF16),
            pltpu.VMEM((D, D), BF16),
            pltpu.VMEM((D, D), BF16),
            pltpu.VMEM((D, D), BF16),
            pltpu.VMEM((D, FF), BF16),
            pltpu.VMEM((D, FF), BF16),
            pltpu.VMEM((FF, D), BF16),
            pltpu.VMEM((9, D, D), BF16),
            pltpu.VMEM((SLOTS, CAP, D), BF16),
            pltpu.VMEM((SLOTS, CAP, D), BF16),
            pltpu.VMEM((HEADS, D // 2, POINTS), BF16),
            pltpu.VMEM((POINTS, FF), F32),
            pltpu.VMEM((OFFSETS, SPAN, POINTS), F32),
            pltpu.VMEM((OFFSETS, SPAN, D), BF16),
            pltpu.VMEM((OFFSETS, HEADS, HEAD + 16, SPAN), BF16),
            pltpu.VMEM((2, HEADS, HEAD + 8, HALF), F32),
            pltpu.VMEM((2, HEADS, 8, HALF), F32),
            pltpu.VMEM((LAG + 1, SPAN, HALF), F32),
            pltpu.VMEM((D, HALF), BF16),
            pltpu.VMEM((2, COLS, D), F32),
            pltpu.VMEM((4, COLS + 2 * PAD, D), BF16),
            pltpu.VMEM((D, D), BF16),
            pltpu.SemaphoreType.DMA((28,)),
            pltpu.SemaphoreType.DMA((SLOTS,)),
            pltpu.SemaphoreType.DMA((SLOTS,)),
            pltpu.SemaphoreType.REGULAR((OFFSETS,)),
            pltpu.SemaphoreType.DMA((14,)),
            pltpu.SemaphoreType.DMA((14,)),
        ],
        compiler_params=pltpu.CompilerParams(
            collective_id=0, has_side_effects=True, vmem_limit_bytes=56 * 1024 * 1024
        ),
        name="decoder",
    )(*args)


def solution(mesh):
    return jax.shard_map(
        per_device,
        mesh=mesh,
        in_specs=(
            P("el", "az", None),
            P("el", "az", None),
            P("az", "el", None, None),
            P("az", "el", None, None, None),
            P("el", "az", None),
            P(),
            P(),
            P(),
            P(),
            P(),
            P(),
            P(),
            P(),
        ),
        out_specs=P("el", "az", None),
        check_vma=False,
    )
```

```python
import math

import jax
import jax.numpy as jnp
from jax import lax
from jax.experimental import pallas as pl
from jax.experimental.pallas import tpu as pltpu
from jax.sharding import PartitionSpec as P

D = 256
HEADS = 8
HEAD = D // HEADS
FF = 1024
NEAR = 16
REACH = 2
OFFSETS = 5
CAP = 16
TOK = 128
COLS = 256
EL = 8
AZ = 16
SLOTS = OFFSETS * EL
POINTS = 512
HALF = 256
PAD = 16
FAR = -1e30
GELU_IN = math.sqrt(2.0 / math.pi)
GELU_CUBE = 0.044715 * GELU_IN
MESH = pl.DeviceIdType.MESH
BF16 = jnp.bfloat16
F32 = jnp.float32

SPAN = EL * CAP
ORDER = (2, 1, 3, 0, 4)
FAR_FIRST = (2, 6, 3, 5, 4, 1, 7)
LAG = 8
SKIP_GROUP = 1
OWN = REACH * EL

SEGMENTS = (
    (0, 0, 0, 64, 0),
    (0, 0, 192, 64, 64),
    (0, 1, 0, 64, 128),
    (0, 1, 192, 64, 192),
    (1, 0, 64, 128, 0),
    (1, 1, 64, 128, 128),
)


def nt(a, b):
    return lax.dot_general(a, b, (((1,), (1,)), ((), ())), preferred_element_type=F32)


def nn(a, b):
    return lax.dot_general(a, b, (((1,), (0,)), ((), ())), preferred_element_type=F32)


def inv_rms(x):
    return lax.rsqrt(jnp.mean(x * x, axis=-1, keepdims=True) + 1e-06)


def gelu(u):
    half = BF16(0.5) * u
    return half + half * jnp.tanh(u * (BF16(GELU_IN) + BF16(GELU_CUBE) * (u * u)))


def kernel(
    points_hbm,
    skip_hbm,
    tokens_hbm,
    slots_hbm,
    index_hbm,
    wq_hbm,
    wk_hbm,
    wv_hbm,
    wo_hbm,
    wh_hbm,
    ws_hbm,
    wd_hbm,
    wc_hbm,
    out_ref,
    pts,
    skp,
    tok,
    slt,
    idx,
    wq,
    wk,
    wv,
    wo,
    wh,
    ws,
    wd,
    wc,
    payload,
    recv,
    qmt,
    hs,
    bias,
    kbuf,
    vt,
    acc,
    best,
    scores,
    att,
    joined,
    cin,
    wvt,
    in_sem,
    send_sem,
    recv_sem,
    ready,
    halo_send,
    halo_recv,
):
    az = lax.axis_index("az")
    el = lax.axis_index("el")

    def az_at(step):
        return lax.rem(az + step + AZ, AZ)

    def el_at(step):
        return lax.rem(el + step, EL)

    def load(number, src, dst):
        copy = pltpu.make_async_copy(src, dst, in_sem.at[number])
        copy.start()
        return copy

    tok_in = load(0, tokens_hbm.at[0, 0], tok)
    slt_in = load(1, slots_hbm.at[0, 0], slt)

    place_z, core = lax.rem(lax.div(az, 2), 4), lax.rem(az, 2)
    wrapped = {0: place_z == 0, 1: (place_z == 0) & (core == 0)}
    ahead = {3: (place_z == 3) & (core == 1), 4: place_z == 3}

    def device(j, r):
        return {"az": az_at(j - REACH), "el": el_at(r)}

    barrier = pltpu.get_barrier_semaphore()

    def greet(j, r):
        pl.semaphore_signal(barrier, inc=1, device_id=device(j, r), device_id_type=MESH)

    for r in range(1, EL):
        greet(REACH, r)
    for j in (0, 1):
        greet(j, 0)

        @pl.when(wrapped[j])
        def _():
            for r in range(1, EL):
                greet(j, r)

    for j in (3, 4):

        @pl.when(jnp.logical_not(ahead[j]))
        def _():
            greet(j, 0)

    heard = EL + OFFSETS - 2
    heard = heard + sum(jnp.where(flag, EL - 1, 0) for flag in ahead.values())
    heard = heard - sum(jnp.where(flag, 1, 0) for flag in wrapped.values())

    wq_in = load(2, wq_hbm, wq)
    pts_in = []
    skp_in = []
    for number, (chunk, row, col, width, place) in enumerate(SEGMENTS):
        here = pl.ds(chunk * HALF + place, width)
        pts_in.append(load(3 + number, points_hbm.at[row, pl.ds(col, width)], pts.at[here]))
    idx_in = load(9, index_hbm, idx)
    wv_in = load(23, wv_hbm, wv)
    wk_in = load(22, wk_hbm, wk)

    slt_in.wait()
    tok_in.wait()
    eye = (
        lax.broadcasted_iota(jnp.int32, (NEAR, NEAR), 0)
        == lax.broadcasted_iota(jnp.int32, (NEAR, NEAR), 1)
    ).astype(F32).astype(BF16)
    slot_cols = nt(eye, slt[...].reshape(SLOTS, CAP).astype(F32).astype(BF16))
    lane_id = lax.broadcasted_iota(jnp.int32, (CAP, TOK), 1).astype(F32)
    picks = jnp.concatenate(
        [
            (jnp.broadcast_to(slot_cols[:, s : s + 1], (CAP, TOK)) == lane_id)
            .astype(F32)
            .astype(BF16)
            for s in range(SLOTS)
        ],
        axis=0,
    )
    payload[...] = nn(picks, tok[...]).astype(BF16).reshape(SLOTS, CAP, D)

    def token_copy(j, r):
        f = el_at(r)
        place = j * EL + (EL - r) % EL
        return pltpu.make_async_remote_copy(
            src_ref=payload.at[j * EL + f],
            dst_ref=recv.at[place],
            send_sem=send_sem.at[place],
            recv_sem=recv_sem.at[place],
            device_id=device(j, r),
            device_id_type=MESH,
        )

    def send_block(j, extra=()):
        for r in FAR_FIRST + extra:
            token_copy(j, r).start()

    def vouched(j):
        pl.semaphore_wait(ready.at[OFFSETS - 1 - j], 1)

    def vouch(j):
        pl.semaphore_signal(ready.at[j], inc=1, device_id=device(j, 0), device_id_type=MESH)

    pl.semaphore_wait(barrier, heard)
    for j in (3, 4):
        vouch(j)
    for j in (0, 1):

        @pl.when(jnp.logical_not(wrapped[j]))
        def _():
            vouch(j)
            token_copy(j, 0).start()

    for j in (3, 4):
        token_copy(j, 0).start()
    for r in FAR_FIRST:
        token_copy(REACH, r).start()
    for j in (3, 4):

        @pl.when(jnp.logical_not(ahead[j]))
        def _():
            vouched(j)

        send_block(j)
    for j in (1, 0):

        @pl.when(jnp.logical_not(wrapped[j]))
        def _():
            vouched(j)
            send_block(j)

    def send_wrapped():
        for j in (1, 0):

            @pl.when(wrapped[j])
            def _():
                vouched(j)
                send_block(j, (0,))

    recv[OWN] = payload[REACH * EL + el]

    for number, (chunk, row, col, width, place) in enumerate(SEGMENTS):
        here = pl.ds(chunk * HALF + place, width)
        skp_in.append(load(15 + number, skip_hbm.at[row, pl.ds(col, width)], skp.at[here]))
    ws_in = load(21, ws_hbm, ws)
    wo_in = load(24, wo_hbm, wo)
    wh_in = load(25, wh_hbm, wh)
    wd_in = load(26, wd_hbm, wd)
    wc_in = load(27, wc_hbm, wc)

    wq_in.wait()
    for copy in pts_in:
        copy.wait()
    query_t = (nt(wq[...].T, pts[...]) * (1.0 / math.sqrt(HEAD) / math.log(2.0))).astype(BF16)
    zero_rows = jnp.zeros((HEAD, POINTS), BF16)
    for h in range(HEADS):
        for part in range(4):
            rows = pl.ds(part * HEAD, HEAD)
            if part == h % 4:
                qmt[h, rows, :] = query_t[h * HEAD : (h + 1) * HEAD, :]
            else:
                qmt[h, rows, :] = zero_rows

    idx_in.wait()
    named = jnp.concatenate(
        [idx[row, :, col : col + width] for _, row, col, width, _ in SEGMENTS], axis=1
    )
    away = (lax.shift_right_logical(named, 4) - el) & (EL - 1)
    entries = (named & ~(SPAN - 1)) + away * CAP + (named & (CAP - 1))
    low = entries & (SPAN - 1)
    high = lax.shift_right_logical(entries, 7)
    unit = lax.shift_left(jnp.ones_like(high), high * 5)

    down = lax.broadcasted_iota(jnp.int32, (8, POINTS), 0)
    for block in range(SPAN // 8):
        total = jnp.zeros((8, POINTS), jnp.int32)
        for n in range(NEAR):
            hit = jnp.broadcast_to(low[n : n + 1, :] - block * 8, (8, POINTS)) == down
            total = total + jnp.where(hit, jnp.broadcast_to(unit[n : n + 1, :], (8, POINTS)), 0)
        for group in range(OFFSETS):
            count = lax.shift_right_logical(total, 5 * group) & 31
            bias[group, pl.ds(block * 8, 8), :] = jnp.maximum(jnp.log2(count.astype(F32)), FAR)

    send_wrapped()

    wv_in.wait()
    wvt[...] = wv[...].T
    for group in range(OFFSETS):
        vt[group, :, pl.ds(HEAD, 16), :] = jnp.ones((HEADS, 16, SPAN), BF16)

    @pl.when(el == 0)
    def _():
        cin[0, :, :] = jnp.zeros((COLS + 2 * PAD, D), BF16)

    @pl.when(el == EL - 1)
    def _():
        cin[3, :, :] = jnp.zeros((COLS + 2 * PAD, D), BF16)

    wk_in.wait()

    def project(group):
        for place in range(EL):
            if group * EL + place != OWN:
                token_copy(group, (EL - place) % EL).wait_recv()
        rows = recv[pl.ds(group * EL, EL)].reshape(SPAN, D)
        kbuf[group] = nn(rows, wk[...]).astype(BF16)
        wide = rows.astype(F32)
        normed_tokens = (wide * inv_rms(wide)).astype(BF16)
        value_t = nt(wvt[...], normed_tokens).astype(BF16)
        for h in range(HEADS):
            vt[group, h, pl.ds(0, HEAD), :] = value_t[h * HEAD : (h + 1) * HEAD, :]

    pending = []
    begun = [0]

    def begin(group, chunk, h):
        span = pl.ds(chunk * HALF, HALF)
        lanes = pl.ds((h // 4) * 128, 128)
        slot = begun[0] % (LAG + 1)
        begun[0] += 1
        raw = nn(kbuf[group, :, lanes], qmt[h, :, span]) + bias[group, :, span]
        scores[slot] = raw
        top = jnp.max(raw, axis=0, keepdims=True)
        fade = None
        if group != ORDER[0]:
            old = best[chunk, h][:1, :]
            top = jnp.maximum(old, top)
            fade = jnp.exp2(old - top)
        if group != ORDER[-1]:
            best[chunk, h] = jnp.broadcast_to(top, (8, HALF))
        pending.append((group, chunk, h, slot, top, fade))

    def finish():
        group, chunk, h, slot, top, fade = pending.pop(0)
        weights = jnp.exp2((scores[slot] - top).astype(BF16))
        summed = nn(vt[group, h], weights)[: HEAD + 8, :]
        if group != ORDER[0]:
            summed = summed + acc[chunk, h] * fade
        acc[chunk, h] = summed

    def halo(number, src, dst, device):
        return pltpu.make_async_remote_copy(
            src_ref=src,
            dst_ref=dst,
            send_sem=halo_send.at[number],
            recv_sem=halo_recv.at[number],
            device_id=device,
            device_id_type=MESH,
        )

    west, east = az_at(-1), az_at(1)
    above = jnp.maximum(el - 1, 0)
    below = jnp.minimum(el + 1, EL - 1)
    first, last = pl.ds(PAD, PAD), pl.ds(COLS, PAD)
    left_pad, right_pad = pl.ds(0, PAD), pl.ds(PAD + COLS, PAD)

    def row_copies(chunk, row):
        number = 5 * row
        mine, theirs = (1, 3) if row == 0 else (2, 0)
        there = above if row == 0 else below
        if chunk == 1:
            mid = pl.ds(PAD + 64, 128)
            return [halo(number, cin.at[mine, mid], cin.at[theirs, mid], {"az": az, "el": there})]
        one, two = pl.ds(PAD, 64), pl.ds(PAD + 192, 64)
        return [
            halo(number + 1, cin.at[mine, one], cin.at[theirs, one], {"az": az, "el": there}),
            halo(number + 2, cin.at[mine, two], cin.at[theirs, two], {"az": az, "el": there}),
            halo(
                number + 3, cin.at[mine, first], cin.at[theirs, right_pad], {"az": west, "el": there}
            ),
            halo(
                number + 4, cin.at[mine, last], cin.at[theirs, left_pad], {"az": east, "el": there}
            ),
        ]

    def side_copies():
        return [
            halo(10, cin.at[1, first], cin.at[1, right_pad], {"az": west, "el": el}),
            halo(11, cin.at[2, first], cin.at[2, right_pad], {"az": west, "el": el}),
            halo(12, cin.at[1, last], cin.at[1, left_pad], {"az": east, "el": el}),
            halo(13, cin.at[2, last], cin.at[2, left_pad], {"az": east, "el": el}),
        ]

    def sends_row(row):
        return (el > 0) if row == 0 else (el < EL - 1)

    def join(chunk, parts):
        for h in range(HEADS):
            share = acc[chunk, h, :HEAD, :] * (1.0 / acc[chunk, h, HEAD : HEAD + 1, :])
            att[pl.ds(h * HEAD, HEAD), :] = share.astype(BF16)
        attended = att[...].T
        for rows in parts:
            begin_at, size = min(rows) * 128, len(rows) * 128
            span = pl.ds(chunk * HALF + begin_at, size)
            residual = pts[span, :].astype(F32) + nn(
                attended[begin_at : begin_at + size, :], wo[...]
            )
            normed = (residual * inv_rms(residual)).astype(BF16)
            total = residual
            for block in range(FF // D):
                cols = pl.ds(block * D, D)
                hidden = gelu((nn(normed, wh[:, cols]) + hs[span, cols]).astype(BF16))
                total = total + nn(hidden, wd[cols, :])
            conv_in = (total * inv_rms(total)).astype(BF16)
            for c, row, col, width, place in SEGMENTS:
                if c == chunk and row in rows:
                    start = place - begin_at
                    joined[row, pl.ds(col, width), :] = total[start : start + width, :]
                    cin[1 + row, pl.ds(PAD + col, width), :] = conv_in[start : start + width, :]
            for _ in range(len(pending) * len(rows) // 2):
                finish()
            for row in rows:

                @pl.when(sends_row(row))
                def _():
                    for copy in row_copies(chunk, row):
                        copy.start()

        if chunk == 0:
            for copy in side_copies():
                copy.start()

    def skip_part(block):
        cols = pl.ds(block * D, D)
        hs[:, cols] = nn(skp[...], ws[:, cols])

    for group in ORDER[:-1]:
        project(group)
        if group == SKIP_GROUP:
            for copy in skp_in:
                copy.wait()
            ws_in.wait()
        for chunk in range(2):
            for h in range(HEADS):
                begin(group, chunk, h)
                if len(pending) > LAG:
                    finish()
                if group == SKIP_GROUP and h % 4 == 3:
                    skip_part(2 * chunk + h // 4)
    while pending:
        finish()

    wo_in.wait()
    wh_in.wait()
    wd_in.wait()
    project(ORDER[-1])
    for chunk in range(2):
        for h in range(HEADS):
            begin(ORDER[-1], chunk, h)
            if chunk == 1:
                finish()
    join(0, ((1, 0),))
    join(1, ((1, 0),))

    for copy in side_copies():
        copy.wait_recv()
    wc_in.wait()

    def taps(row):
        return [cin[row, pl.ds(PAD + step, COLS), :] for step in (-1, 0, 1)]

    own = jnp.concatenate(taps(1) + taps(2), axis=1)
    joined[0] = joined[0] + nn(own, wc[pl.ds(3, 6)].reshape(6 * D, D))
    joined[1] = joined[1] + nn(own, wc[pl.ds(0, 6)].reshape(6 * D, D))

    for j in range(OFFSETS):
        for r in range(EL):
            if (j, r) != (REACH, 0):
                token_copy(j, r).wait_send()
    for copy in side_copies():
        copy.wait_send()

    for row in range(2):

        @pl.when(sends_row(row))
        def _():
            for chunk in range(2):
                for copy in row_copies(chunk, row):
                    copy.wait_send()

    @pl.when(el > 0)
    def _():
        for chunk in range(2):
            for copy in row_copies(chunk, 1):
                copy.wait_recv()

    upper = nn(jnp.concatenate(taps(0), axis=1), wc[pl.ds(0, 3)].reshape(3 * D, D))
    out_ref[0] = (joined[0] + upper).astype(BF16)

    @pl.when(el < EL - 1)
    def _():
        for chunk in range(2):
            for copy in row_copies(chunk, 0):
                copy.wait_recv()

    lower = nn(jnp.concatenate(taps(3), axis=1), wc[pl.ds(6, 3)].reshape(3 * D, D))
    out_ref[1] = (joined[1] + lower).astype(BF16)


def per_device(*args):
    args = args[:4] + (jnp.swapaxes(args[4], 1, 2),) + args[5:]
    any_spec = pl.BlockSpec(memory_space=pl.ANY)
    return pl.pallas_call(
        kernel,
        out_shape=pltpu.VMEM((2, COLS, D), BF16),
        in_specs=[any_spec] * len(args),
        out_specs=pl.BlockSpec(memory_space=pltpu.VMEM),
        scratch_shapes=[
            pltpu.VMEM((POINTS, D), BF16),
            pltpu.VMEM((POINTS, D), BF16),
            pltpu.VMEM((TOK, D), BF16),
            pltpu.VMEM((OFFSETS, EL, CAP), jnp.int32),
            pltpu.VMEM((2, NEAR, COLS), jnp.int32),
            pltpu.VMEM((D, D), BF16),
            pltpu.VMEM((D, D), BF16),
            pltpu.VMEM((D, D), BF16),
            pltpu.VMEM((D, D), BF16),
            pltpu.VMEM((D, FF), BF16),
            pltpu.VMEM((D, FF), BF16),
            pltpu.VMEM((FF, D), BF16),
            pltpu.VMEM((9, D, D), BF16),
            pltpu.VMEM((SLOTS, CAP, D), BF16),
            pltpu.VMEM((SLOTS, CAP, D), BF16),
            pltpu.VMEM((HEADS, D // 2, POINTS), BF16),
            pltpu.VMEM((POINTS, FF), F32),
            pltpu.VMEM((OFFSETS, SPAN, POINTS), F32),
            pltpu.VMEM((OFFSETS, SPAN, D), BF16),
            pltpu.VMEM((OFFSETS, HEADS, HEAD + 16, SPAN), BF16),
            pltpu.VMEM((2, HEADS, HEAD + 8, HALF), F32),
            pltpu.VMEM((2, HEADS, 8, HALF), F32),
            pltpu.VMEM((LAG + 1, SPAN, HALF), F32),
            pltpu.VMEM((D, HALF), BF16),
            pltpu.VMEM((2, COLS, D), F32),
            pltpu.VMEM((4, COLS + 2 * PAD, D), BF16),
            pltpu.VMEM((D, D), BF16),
            pltpu.SemaphoreType.DMA((28,)),
            pltpu.SemaphoreType.DMA((SLOTS,)),
            pltpu.SemaphoreType.DMA((SLOTS,)),
            pltpu.SemaphoreType.REGULAR((OFFSETS,)),
            pltpu.SemaphoreType.DMA((14,)),
            pltpu.SemaphoreType.DMA((14,)),
        ],
        compiler_params=pltpu.CompilerParams(
            collective_id=0, has_side_effects=True, vmem_limit_bytes=56 * 1024 * 1024
        ),
        name="decoder",
    )(*args)


def solution(mesh):
    return jax.shard_map(
        per_device,
        mesh=mesh,
        in_specs=(
            P("el", "az", None),
            P("el", "az", None),
            P("az", "el", None, None),
            P("az", "el", None, None, None),
            P("el", "az", None),
            P(),
            P(),
            P(),
            P(),
            P(),
            P(),
            P(),
            P(),
        ),
        out_specs=P("el", "az", None),
        check_vma=False,
    )
```

```python
import math

import jax
import jax.numpy as jnp
from jax import lax
from jax.experimental import pallas as pl
from jax.experimental.pallas import tpu as pltpu
from jax.sharding import PartitionSpec as P

D = 256
HEADS = 8
HEAD = D // HEADS
FF = 1024
NEAR = 16
REACH = 2
OFFSETS = 5
CAP = 16
TOK = 128
COLS = 256
EL = 8
AZ = 16
SLOTS = OFFSETS * EL
POINTS = 512
HALF = 256
PAD = 16
FAR = -1e30
GELU_IN = math.sqrt(2.0 / math.pi)
GELU_CUBE = 0.044715 * GELU_IN
MESH = pl.DeviceIdType.MESH
BF16 = jnp.bfloat16
F32 = jnp.float32

SPAN = EL * CAP
FAR_FIRST = (2, 6, 3, 5, 4, 1, 7)
LAG = 8
SKIP_STEP = 1
OWN = REACH * EL

SEGMENTS = (
    (0, 0, 0, 64, 0),
    (0, 0, 192, 64, 64),
    (0, 1, 0, 64, 128),
    (0, 1, 192, 64, 192),
    (1, 0, 64, 128, 0),
    (1, 1, 64, 128, 128),
)


def nt(a, b):
    return lax.dot_general(a, b, (((1,), (1,)), ((), ())), preferred_element_type=F32)


def nn(a, b):
    return lax.dot_general(a, b, (((1,), (0,)), ((), ())), preferred_element_type=F32)


def inv_rms(x):
    return lax.rsqrt(jnp.mean(x * x, axis=-1, keepdims=True) + 1e-06)


def gelu(u):
    half = BF16(0.5) * u
    return half + half * jnp.tanh(u * (BF16(GELU_IN) + BF16(GELU_CUBE) * (u * u)))


def kernel(
    points_hbm,
    skip_hbm,
    tokens_hbm,
    slots_hbm,
    index_hbm,
    wq_hbm,
    wk_hbm,
    wv_hbm,
    wo_hbm,
    wh_hbm,
    ws_hbm,
    wd_hbm,
    wc_hbm,
    out_ref,
    pts,
    skp,
    tok,
    slt,
    idx,
    wq,
    wk,
    wv,
    wo,
    wh,
    ws,
    wd,
    wc,
    payload,
    recv,
    qmt,
    hs,
    bias,
    kbuf,
    vt,
    acc,
    best,
    scores,
    att,
    joined,
    cin,
    wvt,
    in_sem,
    send_sem,
    recv_sem,
    ready,
    halo_send,
    halo_recv,
):
    az = lax.axis_index("az")
    el = lax.axis_index("el")

    def az_at(step):
        return lax.rem(az + step + AZ, AZ)

    def el_at(step):
        return lax.rem(el + step, EL)

    def load(number, src, dst):
        copy = pltpu.make_async_copy(src, dst, in_sem.at[number])
        copy.start()
        return copy

    tok_in = load(0, tokens_hbm.at[0, 0], tok)
    slt_in = load(1, slots_hbm.at[0, 0], slt)

    place_z, core = lax.rem(lax.div(az, 2), 4), lax.rem(az, 2)
    wrapped = {0: place_z == 0, 1: (place_z == 0) & (core == 0)}
    ahead = {3: (place_z == 3) & (core == 1), 4: place_z == 3}

    def device(j, r):
        return {"az": az_at(j - REACH), "el": el_at(r)}

    barrier = pltpu.get_barrier_semaphore()

    def greet(j, r):
        pl.semaphore_signal(barrier, inc=1, device_id=device(j, r), device_id_type=MESH)

    for r in range(1, EL):
        greet(REACH, r)
    for j in (0, 1):
        greet(j, 0)

        @pl.when(wrapped[j])
        def _():
            for r in range(1, EL):
                greet(j, r)

    for j in (3, 4):

        @pl.when(jnp.logical_not(ahead[j]))
        def _():
            greet(j, 0)

    heard = EL + OFFSETS - 2
    heard = heard + sum(jnp.where(flag, EL - 1, 0) for flag in ahead.values())
    heard = heard - sum(jnp.where(flag, 1, 0) for flag in wrapped.values())

    wq_in = load(2, wq_hbm, wq)
    pts_in = []
    skp_in = []
    for number, (chunk, row, col, width, place) in enumerate(SEGMENTS):
        here = pl.ds(chunk * HALF + place, width)
        pts_in.append(load(3 + number, points_hbm.at[row, pl.ds(col, width)], pts.at[here]))
    idx_in = load(9, index_hbm, idx)
    wv_in = load(23, wv_hbm, wv)
    wk_in = load(22, wk_hbm, wk)

    slt_in.wait()
    tok_in.wait()
    eye = (
        lax.broadcasted_iota(jnp.int32, (NEAR, NEAR), 0)
        == lax.broadcasted_iota(jnp.int32, (NEAR, NEAR), 1)
    ).astype(F32).astype(BF16)
    slot_cols = nt(eye, slt[...].reshape(SLOTS, CAP).astype(F32).astype(BF16))
    lane_id = lax.broadcasted_iota(jnp.int32, (CAP, TOK), 1).astype(F32)
    picks = jnp.concatenate(
        [
            (jnp.broadcast_to(slot_cols[:, s : s + 1], (CAP, TOK)) == lane_id)
            .astype(F32)
            .astype(BF16)
            for s in range(SLOTS)
        ],
        axis=0,
    )
    payload[...] = nn(picks, tok[...]).astype(BF16).reshape(SLOTS, CAP, D)

    def token_copy(j, r):
        f = el_at(r)
        place = j * EL + (EL - r) % EL
        return pltpu.make_async_remote_copy(
            src_ref=payload.at[j * EL + f],
            dst_ref=recv.at[place],
            send_sem=send_sem.at[place],
            recv_sem=recv_sem.at[place],
            device_id=device(j, r),
            device_id_type=MESH,
        )

    def send_block(j, extra=()):
        for r in FAR_FIRST + extra:
            token_copy(j, r).start()

    def vouched(j):
        pl.semaphore_wait(ready.at[OFFSETS - 1 - j], 1)

    def vouch(j):
        pl.semaphore_signal(ready.at[j], inc=1, device_id=device(j, 0), device_id_type=MESH)

    pl.semaphore_wait(barrier, heard)
    for j in (3, 4):
        vouch(j)
    for j in (0, 1):

        @pl.when(jnp.logical_not(wrapped[j]))
        def _():
            vouch(j)
            token_copy(j, 0).start()

    for j in (3, 4):
        token_copy(j, 0).start()
    for r in FAR_FIRST:
        token_copy(REACH, r).start()
    for j in (3, 4):

        @pl.when(jnp.logical_not(ahead[j]))
        def _():
            vouched(j)

        send_block(j)
    for j in (1, 0):

        @pl.when(jnp.logical_not(wrapped[j]))
        def _():
            vouched(j)
            send_block(j)

    def send_wrapped():
        for j in (1, 0):

            @pl.when(wrapped[j])
            def _():
                vouched(j)
                send_block(j, (0,))

    recv[OWN] = payload[REACH * EL + el]

    for number, (chunk, row, col, width, place) in enumerate(SEGMENTS):
        here = pl.ds(chunk * HALF + place, width)
        skp_in.append(load(15 + number, skip_hbm.at[row, pl.ds(col, width)], skp.at[here]))
    ws_in = load(21, ws_hbm, ws)
    wo_in = load(24, wo_hbm, wo)
    wh_in = load(25, wh_hbm, wh)
    wd_in = load(26, wd_hbm, wd)
    wc_in = load(27, wc_hbm, wc)

    wq_in.wait()
    for copy in pts_in:
        copy.wait()
    query_t = (nt(wq[...].T, pts[...]) * (1.0 / math.sqrt(HEAD) / math.log(2.0))).astype(BF16)
    zero_rows = jnp.zeros((HEAD, POINTS), BF16)
    for h in range(HEADS):
        for part in range(4):
            rows = pl.ds(part * HEAD, HEAD)
            if part == h % 4:
                qmt[h, rows, :] = query_t[h * HEAD : (h + 1) * HEAD, :]
            else:
                qmt[h, rows, :] = zero_rows

    idx_in.wait()
    named = jnp.concatenate(
        [idx[row, :, col : col + width] for _, row, col, width, _ in SEGMENTS], axis=1
    )
    away = (lax.shift_right_logical(named, 4) - el) & (EL - 1)
    entries = (named & ~(SPAN - 1)) + away * CAP + (named & (CAP - 1))
    low = entries & (SPAN - 1)
    high = lax.shift_right_logical(entries, 7)
    unit = lax.shift_left(jnp.ones_like(high), high * 5)

    down = lax.broadcasted_iota(jnp.int32, (8, POINTS), 0)
    for block in range(SPAN // 8):
        total = jnp.zeros((8, POINTS), jnp.int32)
        for n in range(NEAR):
            hit = jnp.broadcast_to(low[n : n + 1, :] - block * 8, (8, POINTS)) == down
            total = total + jnp.where(hit, jnp.broadcast_to(unit[n : n + 1, :], (8, POINTS)), 0)
        for group in range(OFFSETS):
            count = lax.shift_right_logical(total, 5 * group) & 31
            bias[group, pl.ds(block * 8, 8), :] = jnp.maximum(jnp.log2(count.astype(F32)), FAR)

    send_wrapped()

    wv_in.wait()
    wvt[...] = wv[...].T
    for group in range(OFFSETS):
        vt[group, :, pl.ds(HEAD, 16), :] = jnp.ones((HEADS, 16, SPAN), BF16)

    @pl.when(el == 0)
    def _():
        cin[0, :, :] = jnp.zeros((COLS + 2 * PAD, D), BF16)

    @pl.when(el == EL - 1)
    def _():
        cin[3, :, :] = jnp.zeros((COLS + 2 * PAD, D), BF16)

    wk_in.wait()

    starts = (place_z == 0) & (az >= AZ // 2)
    flip = starts & (core == 0)
    order = [REACH]
    for flag, one, two in ((flip, 1, 3), (flip, 3, 1), (starts, 0, 4), (starts, 4, 0)):
        order.append(jnp.where(flag, one, two))

    def project(step):
        group = order[step]
        for place in range(EL):
            if (step, place) != (0, 0):
                token_copy(group, (EL - place) % EL).wait_recv()
        rows = recv[pl.ds(group * EL, EL)].reshape(SPAN, D)
        kbuf[group] = nn(rows, wk[...]).astype(BF16)
        wide = rows.astype(F32)
        normed_tokens = (wide * inv_rms(wide)).astype(BF16)
        value_t = nt(wvt[...], normed_tokens).astype(BF16)
        for h in range(HEADS):
            vt[group, h, pl.ds(0, HEAD), :] = value_t[h * HEAD : (h + 1) * HEAD, :]

    pending = []
    begun = [0]

    def begin(step, chunk, h):
        group = order[step]
        span = pl.ds(chunk * HALF, HALF)
        lanes = pl.ds((h // 4) * 128, 128)
        slot = begun[0] % (LAG + 1)
        begun[0] += 1
        raw = nn(kbuf[group, :, lanes], qmt[h, :, span]) + bias[group, :, span]
        scores[slot] = raw
        top = jnp.max(raw, axis=0, keepdims=True)
        fade = None
        if step > 0:
            old = best[chunk, h][:1, :]
            top = jnp.maximum(old, top)
            fade = jnp.exp2(old - top)
        if step < OFFSETS - 1:
            best[chunk, h] = jnp.broadcast_to(top, (8, HALF))
        pending.append((step, chunk, h, slot, top, fade))

    def finish():
        step, chunk, h, slot, top, fade = pending.pop(0)
        weights = jnp.exp2((scores[slot] - top).astype(BF16))
        summed = nn(vt[order[step], h], weights)[: HEAD + 8, :]
        if step > 0:
            summed = summed + acc[chunk, h] * fade
        acc[chunk, h] = summed

    def halo(number, src, dst, device):
        return pltpu.make_async_remote_copy(
            src_ref=src,
            dst_ref=dst,
            send_sem=halo_send.at[number],
            recv_sem=halo_recv.at[number],
            device_id=device,
            device_id_type=MESH,
        )

    west, east = az_at(-1), az_at(1)
    above = jnp.maximum(el - 1, 0)
    below = jnp.minimum(el + 1, EL - 1)
    first, last = pl.ds(PAD, PAD), pl.ds(COLS, PAD)
    left_pad, right_pad = pl.ds(0, PAD), pl.ds(PAD + COLS, PAD)

    def row_copies(chunk, row):
        number = 5 * row
        mine, theirs = (1, 3) if row == 0 else (2, 0)
        there = above if row == 0 else below
        if chunk == 1:
            mid = pl.ds(PAD + 64, 128)
            return [halo(number, cin.at[mine, mid], cin.at[theirs, mid], {"az": az, "el": there})]
        one, two = pl.ds(PAD, 64), pl.ds(PAD + 192, 64)
        return [
            halo(number + 1, cin.at[mine, one], cin.at[theirs, one], {"az": az, "el": there}),
            halo(number + 2, cin.at[mine, two], cin.at[theirs, two], {"az": az, "el": there}),
            halo(
                number + 3, cin.at[mine, first], cin.at[theirs, right_pad], {"az": west, "el": there}
            ),
            halo(
                number + 4, cin.at[mine, last], cin.at[theirs, left_pad], {"az": east, "el": there}
            ),
        ]

    def side_copies():
        return [
            halo(10, cin.at[1, first], cin.at[1, right_pad], {"az": west, "el": el}),
            halo(11, cin.at[2, first], cin.at[2, right_pad], {"az": west, "el": el}),
            halo(12, cin.at[1, last], cin.at[1, left_pad], {"az": east, "el": el}),
            halo(13, cin.at[2, last], cin.at[2, left_pad], {"az": east, "el": el}),
        ]

    def sends_row(row):
        return (el > 0) if row == 0 else (el < EL - 1)

    def front(chunk):
        for h in range(HEADS):
            share = acc[chunk, h, :HEAD, :] * (1.0 / acc[chunk, h, HEAD : HEAD + 1, :])
            att[chunk, pl.ds(h * HEAD, HEAD), :] = share.astype(BF16)
        span = pl.ds(chunk * HALF, HALF)
        residual = pts[span, :].astype(F32) + nn(att[chunk].T, wo[...])
        return residual, (residual * inv_rms(residual)).astype(BF16)

    def join(chunk, parts, begun, meanwhile=None):
        result = None
        for rows in parts:
            begin_at, size = min(rows) * 128, len(rows) * 128
            span = pl.ds(chunk * HALF + begin_at, size)
            residual, normed = (x[begin_at : begin_at + size, :] for x in begun)
            total = residual
            for block in range(FF // D):
                cols = pl.ds(block * D, D)
                hidden = gelu((nn(normed, wh[:, cols]) + hs[span, cols]).astype(BF16))
                total = total + nn(hidden, wd[cols, :])
            conv_in = (total * inv_rms(total)).astype(BF16)
            for c, row, col, width, place in SEGMENTS:
                if c == chunk and row in rows:
                    start = place - begin_at
                    joined[row, pl.ds(col, width), :] = total[start : start + width, :]
                    cin[1 + row, pl.ds(PAD + col, width), :] = conv_in[start : start + width, :]
            if meanwhile is not None:
                result = meanwhile()
            for row in rows:

                @pl.when(sends_row(row))
                def _():
                    for copy in row_copies(chunk, row):
                        copy.start()

        if chunk == 0:
            for copy in side_copies():
                copy.start()
        return result

    def skip_part(block):
        cols = pl.ds(block * D, D)
        hs[:, cols] = nn(skp[...], ws[:, cols])

    for step in range(OFFSETS - 1):
        project(step)
        if step == SKIP_STEP:
            for copy in skp_in:
                copy.wait()
            ws_in.wait()
        for chunk in range(2):
            for h in range(HEADS):
                begin(step, chunk, h)
                if len(pending) > LAG:
                    finish()
                if step == SKIP_STEP and h % 4 == 3:
                    skip_part(2 * chunk + h // 4)
    while pending:
        finish()

    wo_in.wait()
    wh_in.wait()
    wd_in.wait()
    project(OFFSETS - 1)
    for chunk in range(2):
        for h in range(HEADS):
            begin(OFFSETS - 1, chunk, h)
            if chunk == 1:
                finish()

    def second():
        while pending:
            finish()
        return front(1)

    begun_second = join(0, ((1, 0),), front(0), second)
    join(1, ((1, 0),), begun_second)

    for copy in side_copies():
        copy.wait_recv()
    wc_in.wait()

    def taps(row):
        return [cin[row, pl.ds(PAD + step, COLS), :] for step in (-1, 0, 1)]

    own = jnp.concatenate(taps(1) + taps(2), axis=1)
    joined[0] = joined[0] + nn(own, wc[pl.ds(3, 6)].reshape(6 * D, D))
    joined[1] = joined[1] + nn(own, wc[pl.ds(0, 6)].reshape(6 * D, D))

    for j in range(OFFSETS):
        for r in range(EL):
            if (j, r) != (REACH, 0):
                token_copy(j, r).wait_send()
    for copy in side_copies():
        copy.wait_send()

    for row in range(2):

        @pl.when(sends_row(row))
        def _():
            for chunk in range(2):
                for copy in row_copies(chunk, row):
                    copy.wait_send()

    for step in range(2):
        row = jnp.where(el == EL // 2 - 1, step, 1 - step)

        @pl.when((row == 0) & (el > 0))
        def _():
            for chunk in range(2):
                for copy in row_copies(chunk, 1):
                    copy.wait_recv()

        @pl.when((row == 1) & (el < EL - 1))
        def _():
            for chunk in range(2):
                for copy in row_copies(chunk, 0):
                    copy.wait_recv()

        beyond = jnp.concatenate(taps(3 * row), axis=1)
        matrix = wc[pl.ds(6 * row, 3)].reshape(3 * D, D)
        out_ref[row] = (joined[row] + nn(beyond, matrix)).astype(BF16)


def per_device(*args):
    args = args[:4] + (jnp.swapaxes(args[4], 1, 2),) + args[5:]
    any_spec = pl.BlockSpec(memory_space=pl.ANY)
    return pl.pallas_call(
        kernel,
        out_shape=pltpu.VMEM((2, COLS, D), BF16),
        in_specs=[any_spec] * len(args),
        out_specs=pl.BlockSpec(memory_space=pltpu.VMEM),
        scratch_shapes=[
            pltpu.VMEM((POINTS, D), BF16),
            pltpu.VMEM((POINTS, D), BF16),
            pltpu.VMEM((TOK, D), BF16),
            pltpu.VMEM((OFFSETS, EL, CAP), jnp.int32),
            pltpu.VMEM((2, NEAR, COLS), jnp.int32),
            pltpu.VMEM((D, D), BF16),
            pltpu.VMEM((D, D), BF16),
            pltpu.VMEM((D, D), BF16),
            pltpu.VMEM((D, D), BF16),
            pltpu.VMEM((D, FF), BF16),
            pltpu.VMEM((D, FF), BF16),
            pltpu.VMEM((FF, D), BF16),
            pltpu.VMEM((9, D, D), BF16),
            pltpu.VMEM((SLOTS, CAP, D), BF16),
            pltpu.VMEM((SLOTS, CAP, D), BF16),
            pltpu.VMEM((HEADS, D // 2, POINTS), BF16),
            pltpu.VMEM((POINTS, FF), F32),
            pltpu.VMEM((OFFSETS, SPAN, POINTS), F32),
            pltpu.VMEM((OFFSETS, SPAN, D), BF16),
            pltpu.VMEM((OFFSETS, HEADS, HEAD + 16, SPAN), BF16),
            pltpu.VMEM((2, HEADS, HEAD + 8, HALF), F32),
            pltpu.VMEM((2, HEADS, 8, HALF), F32),
            pltpu.VMEM((LAG + 1, SPAN, HALF), F32),
            pltpu.VMEM((2, D, HALF), BF16),
            pltpu.VMEM((2, COLS, D), F32),
            pltpu.VMEM((4, COLS + 2 * PAD, D), BF16),
            pltpu.VMEM((D, D), BF16),
            pltpu.SemaphoreType.DMA((28,)),
            pltpu.SemaphoreType.DMA((SLOTS,)),
            pltpu.SemaphoreType.DMA((SLOTS,)),
            pltpu.SemaphoreType.REGULAR((OFFSETS,)),
            pltpu.SemaphoreType.DMA((14,)),
            pltpu.SemaphoreType.DMA((14,)),
        ],
        compiler_params=pltpu.CompilerParams(
            collective_id=0, has_side_effects=True, vmem_limit_bytes=56 * 1024 * 1024
        ),
        name="decoder",
    )(*args)


def solution(mesh):
    return jax.shard_map(
        per_device,
        mesh=mesh,
        in_specs=(
            P("el", "az", None),
            P("el", "az", None),
            P("az", "el", None, None),
            P("az", "el", None, None, None),
            P("el", "az", None),
            P(),
            P(),
            P(),
            P(),
            P(),
            P(),
            P(),
            P(),
        ),
        out_specs=P("el", "az", None),
        check_vma=False,
    )
```

```python
import math

import jax
import jax.numpy as jnp
from jax import lax
from jax.experimental import pallas as pl
from jax.experimental.pallas import tpu as pltpu
from jax.sharding import PartitionSpec as P

D = 256
HEADS = 8
HEAD = D // HEADS
FF = 1024
NEAR = 16
REACH = 2
OFFSETS = 5
CAP = 16
TOK = 128
COLS = 256
EL = 8
AZ = 16
SLOTS = OFFSETS * EL
POINTS = 512
HALF = 256
PAD = 16
FAR = -1e30
GELU_IN = math.sqrt(2.0 / math.pi)
GELU_CUBE = 0.044715 * GELU_IN
MESH = pl.DeviceIdType.MESH
BF16 = jnp.bfloat16
F32 = jnp.float32

SPAN = EL * CAP
FAR_FIRST = (2, 6, 3, 5, 4, 1, 7)
LAG = 8
SKIP_STEP = 1
OWN = REACH * EL

SEGMENTS = (
    (0, 0, 0, 64, 0),
    (0, 0, 192, 64, 64),
    (0, 1, 0, 64, 128),
    (0, 1, 192, 64, 192),
    (1, 0, 64, 128, 0),
    (1, 1, 64, 128, 128),
)


def nt(a, b):
    return lax.dot_general(a, b, (((1,), (1,)), ((), ())), preferred_element_type=F32)


def nn(a, b):
    return lax.dot_general(a, b, (((1,), (0,)), ((), ())), preferred_element_type=F32)


def inv_rms(x):
    return lax.rsqrt(jnp.mean(x * x, axis=-1, keepdims=True) + 1e-06)


def gelu(u):
    half = BF16(0.5) * u
    return half + half * jnp.tanh(u * (BF16(GELU_IN) + BF16(GELU_CUBE) * (u * u)))


def kernel(
    points_hbm,
    skip_hbm,
    tokens_hbm,
    slots_hbm,
    index_hbm,
    wq_hbm,
    wk_hbm,
    wv_hbm,
    wo_hbm,
    wh_hbm,
    ws_hbm,
    wd_hbm,
    wc_hbm,
    out_ref,
    pts,
    skp,
    tok,
    slt,
    idx,
    wq,
    wk,
    wv,
    wo,
    wh,
    ws,
    wd,
    wc,
    payload,
    recv,
    qmt,
    hs,
    bias,
    kbuf,
    vt,
    acc,
    best,
    scores,
    att,
    joined,
    cin,
    wvt,
    in_sem,
    send_sem,
    recv_sem,
    ready,
    halo_send,
    halo_recv,
):
    az = lax.axis_index("az")
    el = lax.axis_index("el")

    def az_at(step):
        return lax.rem(az + step + AZ, AZ)

    def el_at(step):
        return lax.rem(el + step, EL)

    def load(number, src, dst):
        copy = pltpu.make_async_copy(src, dst, in_sem.at[number])
        copy.start()
        return copy

    tok_in = load(0, tokens_hbm.at[0, 0], tok)
    slt_in = load(1, slots_hbm.at[0, 0], slt)

    place_z, core = lax.rem(lax.div(az, 2), 4), lax.rem(az, 2)
    wrapped = {0: place_z == 0, 1: (place_z == 0) & (core == 0)}
    ahead = {3: (place_z == 3) & (core == 1), 4: place_z == 3}

    def device(j, r):
        return {"az": az_at(j - REACH), "el": el_at(r)}

    barrier = pltpu.get_barrier_semaphore()

    def greet(j, r):
        pl.semaphore_signal(barrier, inc=1, device_id=device(j, r), device_id_type=MESH)

    for r in range(1, EL):
        greet(REACH, r)
    for j in (0, 1):
        greet(j, 0)

        @pl.when(wrapped[j])
        def _():
            for r in range(1, EL):
                greet(j, r)

    for j in (3, 4):

        @pl.when(jnp.logical_not(ahead[j]))
        def _():
            greet(j, 0)

    heard = EL + OFFSETS - 2
    heard = heard + sum(jnp.where(flag, EL - 1, 0) for flag in ahead.values())
    heard = heard - sum(jnp.where(flag, 1, 0) for flag in wrapped.values())

    wq_in = load(2, wq_hbm, wq)
    pts_in = []
    skp_in = []
    for number, (chunk, row, col, width, place) in enumerate(SEGMENTS):
        here = pl.ds(chunk * HALF + place, width)
        pts_in.append(load(3 + number, points_hbm.at[row, pl.ds(col, width)], pts.at[here]))
    idx_in = load(9, index_hbm, idx)
    wv_in = load(23, wv_hbm, wv)
    wk_in = load(22, wk_hbm, wk)

    slt_in.wait()
    tok_in.wait()
    eye = (
        lax.broadcasted_iota(jnp.int32, (NEAR, NEAR), 0)
        == lax.broadcasted_iota(jnp.int32, (NEAR, NEAR), 1)
    ).astype(F32).astype(BF16)
    slot_cols = nt(eye, slt[...].reshape(SLOTS, CAP).astype(F32).astype(BF16))
    lane_id = lax.broadcasted_iota(jnp.int32, (CAP, TOK), 1).astype(F32)
    picks = jnp.concatenate(
        [
            (jnp.broadcast_to(slot_cols[:, s : s + 1], (CAP, TOK)) == lane_id)
            .astype(F32)
            .astype(BF16)
            for s in range(SLOTS)
        ],
        axis=0,
    )
    payload[...] = nn(picks, tok[...]).astype(BF16).reshape(SLOTS, CAP, D)

    def token_copy(j, r):
        f = el_at(r)
        place = j * EL + (EL - r) % EL
        return pltpu.make_async_remote_copy(
            src_ref=payload.at[j * EL + f],
            dst_ref=recv.at[place],
            send_sem=send_sem.at[place],
            recv_sem=recv_sem.at[place],
            device_id=device(j, r),
            device_id_type=MESH,
        )

    def send_block(j, extra=()):
        for r in FAR_FIRST + extra:
            token_copy(j, r).start()

    def vouched(j):
        pl.semaphore_wait(ready.at[OFFSETS - 1 - j], 1)

    def vouch(j):
        pl.semaphore_signal(ready.at[j], inc=1, device_id=device(j, 0), device_id_type=MESH)

    pl.semaphore_wait(barrier, heard)
    for j in (3, 4):
        vouch(j)
    for j in (0, 1):

        @pl.when(jnp.logical_not(wrapped[j]))
        def _():
            vouch(j)
            token_copy(j, 0).start()

    for j in (3, 4):
        token_copy(j, 0).start()
    for r in FAR_FIRST:
        token_copy(REACH, r).start()
    for j in (3, 4):

        @pl.when(jnp.logical_not(ahead[j]))
        def _():
            vouched(j)

        send_block(j)
    for j in (1, 0):

        @pl.when(jnp.logical_not(wrapped[j]))
        def _():
            vouched(j)
            send_block(j)

    def send_wrapped():
        for j in (1, 0):

            @pl.when(wrapped[j])
            def _():
                vouched(j)
                send_block(j, (0,))

    recv[OWN] = payload[REACH * EL + el]

    for number, (chunk, row, col, width, place) in enumerate(SEGMENTS):
        here = pl.ds(chunk * HALF + place, width)
        skp_in.append(load(15 + number, skip_hbm.at[row, pl.ds(col, width)], skp.at[here]))
    ws_in = load(21, ws_hbm, ws)
    wo_in = load(24, wo_hbm, wo)
    wh_in = load(25, wh_hbm, wh)
    wd_in = load(26, wd_hbm, wd)
    wc_in = load(27, wc_hbm, wc)

    wq_in.wait()
    for copy in pts_in:
        copy.wait()
    query_t = (nt(wq[...].T, pts[...]) * (1.0 / math.sqrt(HEAD) / math.log(2.0))).astype(BF16)
    zero_rows = jnp.zeros((HEAD, POINTS), BF16)
    for h in range(HEADS):
        for part in range(4):
            rows = pl.ds(part * HEAD, HEAD)
            if part == h % 4:
                qmt[h, rows, :] = query_t[h * HEAD : (h + 1) * HEAD, :]
            else:
                qmt[h, rows, :] = zero_rows

    idx_in.wait()
    named = jnp.concatenate(
        [idx[row, :, col : col + width] for _, row, col, width, _ in SEGMENTS], axis=1
    )
    away = (lax.shift_right_logical(named, 4) - el) & (EL - 1)
    entries = (named & ~(SPAN - 1)) + away * CAP + (named & (CAP - 1))
    low = entries & (SPAN - 1)
    high = lax.shift_right_logical(entries, 7)
    unit = lax.shift_left(jnp.ones_like(high), high * 5)

    down = lax.broadcasted_iota(jnp.int32, (8, POINTS), 0)
    for block in range(SPAN // 8):
        total = jnp.zeros((8, POINTS), jnp.int32)
        for n in range(NEAR):
            hit = jnp.broadcast_to(low[n : n + 1, :] - block * 8, (8, POINTS)) == down
            total = total + jnp.where(hit, jnp.broadcast_to(unit[n : n + 1, :], (8, POINTS)), 0)
        for group in range(OFFSETS):
            count = lax.shift_right_logical(total, 5 * group) & 31
            bias[group, pl.ds(block * 8, 8), :] = jnp.maximum(jnp.log2(count.astype(F32)), FAR)

    send_wrapped()

    wv_in.wait()
    wvt[...] = wv[...].T
    for group in range(OFFSETS):
        vt[group, :, pl.ds(HEAD, 16), :] = jnp.ones((HEADS, 16, SPAN), BF16)

    @pl.when(el == 0)
    def _():
        cin[0, :, :] = jnp.zeros((COLS + 2 * PAD, D), BF16)

    @pl.when(el == EL - 1)
    def _():
        cin[3, :, :] = jnp.zeros((COLS + 2 * PAD, D), BF16)

    wk_in.wait()

    starts = (place_z == 0) & (az >= AZ // 2)
    flip = starts & (core == 0)
    order = [REACH]
    for flag, one, two in ((flip, 1, 3), (flip, 3, 1), (starts, 0, 4), (starts, 4, 0)):
        order.append(jnp.where(flag, one, two))

    def project(step):
        group = order[step]
        for place in range(EL):
            if (step, place) != (0, 0):
                token_copy(group, (EL - place) % EL).wait_recv()
        rows = recv[pl.ds(group * EL, EL)].reshape(SPAN, D)
        kbuf[group] = nn(rows, wk[...]).astype(BF16)
        wide = rows.astype(F32)
        normed_tokens = (wide * inv_rms(wide)).astype(BF16)
        value_t = nt(wvt[...], normed_tokens).astype(BF16)
        for h in range(HEADS):
            vt[group, h, pl.ds(0, HEAD), :] = value_t[h * HEAD : (h + 1) * HEAD, :]

    pending = []
    begun = [0]

    def begin(step, chunk, h):
        group = order[step]
        span = pl.ds(chunk * HALF, HALF)
        lanes = pl.ds((h // 4) * 128, 128)
        slot = begun[0] % (LAG + 1)
        begun[0] += 1
        raw = nn(kbuf[group, :, lanes], qmt[h, :, span]) + bias[group, :, span]
        scores[slot] = raw
        top = jnp.max(raw, axis=0, keepdims=True)
        fade = None
        if step > 0:
            old = best[chunk, h][:1, :]
            top = jnp.maximum(old, top)
            fade = jnp.exp2(old - top)
        if step < OFFSETS - 1:
            best[chunk, h] = jnp.broadcast_to(top, (8, HALF))
        pending.append((step, chunk, h, slot, top, fade))

    def finish():
        step, chunk, h, slot, top, fade = pending.pop(0)
        weights = jnp.exp2((scores[slot] - top).astype(BF16))
        summed = nn(vt[order[step], h], weights)[: HEAD + 8, :]
        if step > 0:
            summed = summed + acc[chunk, h] * fade
        acc[chunk, h] = summed

    def halo(number, src, dst, device):
        return pltpu.make_async_remote_copy(
            src_ref=src,
            dst_ref=dst,
            send_sem=halo_send.at[number],
            recv_sem=halo_recv.at[number],
            device_id=device,
            device_id_type=MESH,
        )

    west, east = az_at(-1), az_at(1)
    above = jnp.maximum(el - 1, 0)
    below = jnp.minimum(el + 1, EL - 1)
    first, last = pl.ds(PAD, PAD), pl.ds(COLS, PAD)
    left_pad, right_pad = pl.ds(0, PAD), pl.ds(PAD + COLS, PAD)

    def row_copies(chunk, row):
        number = 5 * row
        mine, theirs = (1, 3) if row == 0 else (2, 0)
        there = above if row == 0 else below
        if chunk == 1:
            mid = pl.ds(PAD + 64, 128)
            return [halo(number, cin.at[mine, mid], cin.at[theirs, mid], {"az": az, "el": there})]
        one, two = pl.ds(PAD, 64), pl.ds(PAD + 192, 64)
        return [
            halo(number + 1, cin.at[mine, one], cin.at[theirs, one], {"az": az, "el": there}),
            halo(number + 2, cin.at[mine, two], cin.at[theirs, two], {"az": az, "el": there}),
            halo(
                number + 3, cin.at[mine, first], cin.at[theirs, right_pad], {"az": west, "el": there}
            ),
            halo(
                number + 4, cin.at[mine, last], cin.at[theirs, left_pad], {"az": east, "el": there}
            ),
        ]

    def side_copies():
        return [
            halo(10, cin.at[1, first], cin.at[1, right_pad], {"az": west, "el": el}),
            halo(11, cin.at[2, first], cin.at[2, right_pad], {"az": west, "el": el}),
            halo(12, cin.at[1, last], cin.at[1, left_pad], {"az": east, "el": el}),
            halo(13, cin.at[2, last], cin.at[2, left_pad], {"az": east, "el": el}),
        ]

    def sends_row(row):
        return (el > 0) if row == 0 else (el < EL - 1)

    def front(chunk):
        for h in range(HEADS):
            share = acc[chunk, h, :HEAD, :] * (1.0 / acc[chunk, h, HEAD : HEAD + 1, :])
            att[chunk, pl.ds(h * HEAD, HEAD), :] = share.astype(BF16)
        span = pl.ds(chunk * HALF, HALF)
        residual = pts[span, :].astype(F32) + nn(att[chunk].T, wo[...])
        return residual, (residual * inv_rms(residual)).astype(BF16)

    def join(chunk, parts, begun, meanwhile=None):
        result = None
        for rows in parts:
            begin_at, size = min(rows) * 128, len(rows) * 128
            span = pl.ds(chunk * HALF + begin_at, size)
            residual, normed = (x[begin_at : begin_at + size, :] for x in begun)
            total = residual
            for block in range(FF // D):
                cols = pl.ds(block * D, D)
                hidden = gelu((nn(normed, wh[:, cols]) + hs[span, cols]).astype(BF16))
                total = total + nn(hidden, wd[cols, :])
            conv_in = (total * inv_rms(total)).astype(BF16)
            for c, row, col, width, place in SEGMENTS:
                if c == chunk and row in rows:
                    start = place - begin_at
                    joined[row, pl.ds(col, width), :] = total[start : start + width, :]
                    cin[1 + row, pl.ds(PAD + col, width), :] = conv_in[start : start + width, :]
            if meanwhile is not None and rows == parts[-1]:
                result = meanwhile()
            for row in rows:

                @pl.when(sends_row(row))
                def _():
                    for copy in row_copies(chunk, row):
                        copy.start()

        if chunk == 0:
            for copy in side_copies():
                copy.start()
        return result

    def skip_part(block):
        cols = pl.ds(block * D, D)
        hs[:, cols] = nn(skp[...], ws[:, cols])

    for step in range(OFFSETS - 1):
        project(step)
        if step == SKIP_STEP:
            for copy in skp_in:
                copy.wait()
            ws_in.wait()
        for chunk in range(2):
            for h in range(HEADS):
                begin(step, chunk, h)
                if len(pending) > LAG:
                    finish()
                if step == SKIP_STEP and h % 4 == 3:
                    skip_part(2 * chunk + h // 4)
    while pending:
        finish()

    wo_in.wait()
    wh_in.wait()
    wd_in.wait()
    project(OFFSETS - 1)
    for chunk in range(2):
        for h in range(HEADS):
            begin(OFFSETS - 1, chunk, h)
            if chunk == 1:
                finish()

    def second():
        while pending:
            finish()
        return front(1)

    begun_second = join(0, ((1,), (0,)), front(0), second)
    join(1, ((1, 0),), begun_second)

    for copy in side_copies():
        copy.wait_recv()
    wc_in.wait()

    def taps(row):
        return [cin[row, pl.ds(PAD + step, COLS), :] for step in (-1, 0, 1)]

    own = jnp.concatenate(taps(1) + taps(2), axis=1)
    joined[0] = joined[0] + nn(own, wc[pl.ds(3, 6)].reshape(6 * D, D))
    joined[1] = joined[1] + nn(own, wc[pl.ds(0, 6)].reshape(6 * D, D))

    for j in range(OFFSETS):
        for r in range(EL):
            if (j, r) != (REACH, 0):
                token_copy(j, r).wait_send()
    for copy in side_copies():
        copy.wait_send()

    for row in range(2):

        @pl.when(sends_row(row))
        def _():
            for chunk in range(2):
                for copy in row_copies(chunk, row):
                    copy.wait_send()

    for step in range(2):
        row = jnp.where(el == EL // 2 - 1, step, 1 - step)

        @pl.when((row == 0) & (el > 0))
        def _():
            for chunk in range(2):
                for copy in row_copies(chunk, 1):
                    copy.wait_recv()

        @pl.when((row == 1) & (el < EL - 1))
        def _():
            for chunk in range(2):
                for copy in row_copies(chunk, 0):
                    copy.wait_recv()

        beyond = jnp.concatenate(taps(3 * row), axis=1)
        matrix = wc[pl.ds(6 * row, 3)].reshape(3 * D, D)
        out_ref[row] = (joined[row] + nn(beyond, matrix)).astype(BF16)


def per_device(*args):
    args = args[:4] + (jnp.swapaxes(args[4], 1, 2),) + args[5:]
    any_spec = pl.BlockSpec(memory_space=pl.ANY)
    return pl.pallas_call(
        kernel,
        out_shape=pltpu.VMEM((2, COLS, D), BF16),
        in_specs=[any_spec] * len(args),
        out_specs=pl.BlockSpec(memory_space=pltpu.VMEM),
        scratch_shapes=[
            pltpu.VMEM((POINTS, D), BF16),
            pltpu.VMEM((POINTS, D), BF16),
            pltpu.VMEM((TOK, D), BF16),
            pltpu.VMEM((OFFSETS, EL, CAP), jnp.int32),
            pltpu.VMEM((2, NEAR, COLS), jnp.int32),
            pltpu.VMEM((D, D), BF16),
            pltpu.VMEM((D, D), BF16),
            pltpu.VMEM((D, D), BF16),
            pltpu.VMEM((D, D), BF16),
            pltpu.VMEM((D, FF), BF16),
            pltpu.VMEM((D, FF), BF16),
            pltpu.VMEM((FF, D), BF16),
            pltpu.VMEM((9, D, D), BF16),
            pltpu.VMEM((SLOTS, CAP, D), BF16),
            pltpu.VMEM((SLOTS, CAP, D), BF16),
            pltpu.VMEM((HEADS, D // 2, POINTS), BF16),
            pltpu.VMEM((POINTS, FF), F32),
            pltpu.VMEM((OFFSETS, SPAN, POINTS), F32),
            pltpu.VMEM((OFFSETS, SPAN, D), BF16),
            pltpu.VMEM((OFFSETS, HEADS, HEAD + 16, SPAN), BF16),
            pltpu.VMEM((2, HEADS, HEAD + 8, HALF), F32),
            pltpu.VMEM((2, HEADS, 8, HALF), F32),
            pltpu.VMEM((LAG + 1, SPAN, HALF), F32),
            pltpu.VMEM((2, D, HALF), BF16),
            pltpu.VMEM((2, COLS, D), F32),
            pltpu.VMEM((4, COLS + 2 * PAD, D), BF16),
            pltpu.VMEM((D, D), BF16),
            pltpu.SemaphoreType.DMA((28,)),
            pltpu.SemaphoreType.DMA((SLOTS,)),
            pltpu.SemaphoreType.DMA((SLOTS,)),
            pltpu.SemaphoreType.REGULAR((OFFSETS,)),
            pltpu.SemaphoreType.DMA((14,)),
            pltpu.SemaphoreType.DMA((14,)),
        ],
        compiler_params=pltpu.CompilerParams(
            collective_id=0, has_side_effects=True, vmem_limit_bytes=56 * 1024 * 1024
        ),
        name="decoder",
    )(*args)


def solution(mesh):
    return jax.shard_map(
        per_device,
        mesh=mesh,
        in_specs=(
            P("el", "az", None),
            P("el", "az", None),
            P("az", "el", None, None),
            P("az", "el", None, None, None),
            P("el", "az", None),
            P(),
            P(),
            P(),
            P(),
            P(),
            P(),
            P(),
            P(),
        ),
        out_specs=P("el", "az", None),
        check_vma=False,
    )
```
